32 devices in a mesh: dp: 2 (over y), expert: 16 (over z, x, core).
Axes of the slice: x: 2, y: 2, z: 4, core: 2. Of those that a mesh axis runs over, the one named last changes fastest.
Arguments:
- tokens: bfloat16 [2048, 2048], P('expert', 'dp'), may hold values from -6 to 6
- cotangent: bfloat16 [2048, 2048], P('expert', 'dp'), may hold values from -6 to 6
- routes: int32 [2048, 8], P('expert'), may hold values from 0 to 15, all different within a row; in each aligned block of 128 rows (0 to 127, 128 to 255, ...) at most 72 rows name the same one
- gate_probs: float32 [2048, 8], P('expert'), may hold values from 0.02 to 1
- matching: int32 [16], replicated, may hold values from 0 to 15, as said below
- gate_weight: bfloat16 [16, 2048, 768], P('expert', None, 'dp'), may hold values from -0.125 to 0.125
- up_weight: bfloat16 [16, 2048, 768], P('expert', None, 'dp'), may hold values from -0.125 to 0.125
- down_weight: bfloat16 [16, 768, 2048], P('expert', 'dp'), may hold values from -0.21875 to 0.21875
Outputs:
- layer_out: bfloat16 [2048, 2048], P('expert', 'dp')
- gate_grad: bfloat16 [16, 2048, 768], P('expert', None, 'dp')
- up_grad: bfloat16 [16, 2048, 768], P('expert', None, 'dp')
- down_grad: bfloat16 [16, 768, 2048], P('expert', 'dp')
The draws below stay inside these ranges and needn't reach their ends.
Inputs may be any that keep to these rules, and one draw needn't show every extreme that they name: `routes`: each row names 8 different experts. Within each aligned block of 128 rows no expert is named by more than 72 rows, and in some block some expert is named by exactly 72 rows. The weights of expert e sit in slot matching[e]; matching pairs the slots: matching[matching[e]] = e and matching[e] != e.
All inputs are finite; a program needn't handle non-finite values.
Results may differ from the reference program's by a relative error of at most 0.0065.
Values may be sent and summed in bfloat16 or wider, within the bound.
No kernel may reach another device: no remote copies, remote signals or barrier semaphores. Data moves between devices by JAX's collectives and lax.ppermute only.
A program may use at most 128 MiB of HBM per device.

```python
import math
import jax
import jax.numpy as jnp
import numpy as np
from jax import lax

D = 2048
FF = 768
TOP = 8
TOK_DEV = 128
EXPERTS = 16
TOKENS = 2048
CAP = 72
N_EXPERT = 16


def draw_matching(key, part):
    shuffled = jax.random.permutation(key, EXPERTS).astype(jnp.int32)
    first_half = shuffled[0::2]
    second = shuffled[1::2]
    paired = jnp.zeros((EXPERTS,), jnp.int32).at[first_half].set(second).at[second].set(first_half)
    return paired


def level_of(stream_key, extent, split, low, top_value):
    level, own = 1.0, jax.random.fold_in(stream_key, 6)
    for axis_at, blocks in split:
        draws = jnp.exp(jax.random.uniform(jax.random.fold_in(own, axis_at), (blocks,), jnp.float32, low / len(split), top_value / len(split)))
        level = level * jnp.repeat(draws, extent[axis_at] // blocks).reshape([-1 if axis == axis_at else 1 for axis in range(len(extent))])
    return level


def shared_out(stream_key, own, number, rows, number_of, top, most, lean):
    ranking = jax.random.permutation(stream_key, number_of)
    heavy_load, common = load_shares(number_of, rows * top, most, lean, True), load_shares(number_of, rows * top, most, lean, False)
    places = jnp.arange(number_of)

    def named(sizes, offset_by):
        used = int((sizes > 0).sum())
        fixed = max(1, used // 4)
        moved = fixed + (places - fixed + offset_by * (used - fixed)) % max(1, number_of - fixed)
        return jnp.zeros((number_of,), jnp.int32).at[ranking[jnp.where(places < fixed, places, moved)]].set(jnp.asarray(sizes, jnp.int32))

    sizes = jnp.where(number % 4 == 0, named(heavy_load, number // 4), named(common, number - number // 4 - 1))
    mixed = jax.random.permutation(jax.random.fold_in(own, 3), number_of)
    source_of, taker = mixed[0:number_of // 2 * 2:2], mixed[1:number_of // 2 * 2:2]
    slack = jnp.minimum(sizes[source_of] - 1, most - sizes[taker]) // 2
    slack = jnp.where((source_of == ranking[0]) | (taker == ranking[0]) | (sizes[taker] == 0), 0, jnp.maximum(slack, 0))
    moved = jax.random.randint(jax.random.fold_in(own, 4), (number_of // 2,), 0, 1 << 20) % (slack + 1)
    sizes = sizes.at[source_of].add(-moved).at[taker].add(moved)
    labels = jnp.searchsorted(jnp.cumsum(sizes), jnp.arange(rows * top), side="right").astype(jnp.int32)
    table = labels.reshape(top, rows).T
    table = table[jax.random.permutation(jax.random.fold_in(own, 1), rows)]
    offset_by = jax.random.randint(jax.random.fold_in(own, 2), (rows, 1), 0, top)
    return jnp.take_along_axis(table, (jnp.arange(top)[None, :] + offset_by) % top, axis=1)


def load_shares(number_of, total, most, skew, full):
    loads = [(1 << 20) // math.isqrt(grade ** skew) + 1 for grade in range(1, number_of + 1)]
    largest = most if full else min(most, max(-(-total // number_of), total * loads[0] // sum(loads)))
    least = 1 if total - largest >= number_of - 1 else 0
    given, rest = [largest] + [least] * (number_of - 1), total - largest - least * (number_of - 1)
    while rest > 0:
        free = [i for i in range(1, number_of) if given[i] < largest] or [i for i in range(1, number_of) if given[i] < most]
        mass, budget = sum([loads[i] for i in free]), rest
        for i in free:
            extra = min(most - given[i], max(1, budget * loads[i] // mass), rest)
            given[i] = given[i] + extra
            rest = rest - extra
    return np.array(given)


def centred(stream_key, shape, spread, bound, cuts=(), kind=jnp.bfloat16):
    drawn = spread * jax.random.normal(stream_key, shape, jnp.float32)
    if cuts:
        drawn = drawn * level_of(stream_key, shape, cuts, -0.22, 0.18)
    return jnp.clip(drawn, -bound, bound).astype(kind)


def setup_inputs(seed: int = 0) -> dict:
    arg_keys = jax.random.split(jax.random.key(seed), 9)
    tokens = centred(arg_keys[0], (TOKENS, D), 1.0, 6.0, ((0, 16), (1, 2)))
    cotangent = centred(arg_keys[1], (TOKENS, D), 1.0, 6.0, ((0, 16), (1, 2)))
    routes_keys = jax.random.split(jax.random.fold_in(arg_keys[2], 1), TOKENS // TOK_DEV)
    routes_turns = jax.random.permutation(jax.random.fold_in(arg_keys[2], 3), TOKENS // TOK_DEV)
    routes = jax.vmap(lambda own, number: shared_out(jax.random.fold_in(arg_keys[2], 2), own, number, TOK_DEV, EXPERTS, TOP, CAP, 2))(routes_keys, routes_turns).reshape((TOKENS, TOP))
    gate_probs = jnp.clip(jnp.exp(math.log(1.0) - 3.912023 * jax.random.uniform(arg_keys[3], (TOKENS, TOP), jnp.float32) ** level_of(arg_keys[3], (TOKENS, TOP), ((0, 16),), -0.2, 0.2)), 0.02, 1.0)
    matching = draw_matching(jax.random.fold_in(arg_keys[8], 71), 0)
    gate_weight = centred(arg_keys[5], (EXPERTS, D, FF), D ** -0.5, 0.125, ((0, 16), (2, 2)))
    up_weight = centred(arg_keys[6], (EXPERTS, D, FF), D ** -0.5, 0.125, ((0, 16), (2, 2)))
    down_weight = centred(arg_keys[7], (EXPERTS, FF, D), FF ** -0.5, 0.21875, ((0, 16), (1, 2)))
    return {"tokens": tokens, "cotangent": cotangent, "routes": routes, "gate_probs": gate_probs, "matching": matching, "gate_weight": gate_weight, "up_weight": up_weight, "down_weight": down_weight}


def rounded(values):
    return lax.optimization_barrier(values.astype(jnp.bfloat16)).astype(jnp.float32)


def block_table(block_routes, matching):
    flat_routes = block_routes.reshape(-1)
    host_of = matching[flat_routes].astype(jnp.int32)
    host_hit = (host_of[:, None] == jnp.arange(N_EXPERT, dtype=jnp.int32)[None, :]).astype(jnp.int32)
    running = jnp.cumsum(host_hit, axis=0).astype(jnp.int32)
    slot_rank = jnp.sum((running - 1) * host_hit, axis=1).astype(jnp.int32)
    position = (host_of * CAP + slot_rank).astype(jnp.int32)
    empty = jnp.full((N_EXPERT * CAP,), TOK_DEV * TOP, jnp.int32)
    return empty.at[position].set(jnp.arange(TOK_DEV * TOP, dtype=jnp.int32))


def reference(tokens, cotangent, routes, gate_probs, matching, gate_weight, up_weight, down_weight):
    mix_weights = gate_probs / jnp.sum(gate_probs, axis=1, keepdims=True)
    flat_mix = mix_weights.reshape(-1)
    tables = lax.map(lambda block: block_table(block, matching), routes.reshape(N_EXPERT, TOK_DEV, TOP))
    route_count = TOK_DEV * TOP
    half_units = FF // 2

    def one_slot(carry, slot):
        slot_ids = lax.dynamic_slice_in_dim(tables, (slot * CAP).astype(jnp.int32), CAP, 1)
        filled = (slot_ids < route_count).reshape(-1)
        clamped = jnp.minimum(slot_ids, route_count - 1)
        block_base = jnp.arange(N_EXPERT, dtype=jnp.int32)[:, None] * route_count
        route_ids = (block_base + clamped).reshape(-1).astype(jnp.int32)
        token_ids = (route_ids // TOP).astype(jnp.int32)
        gathered = tokens[token_ids]
        rows_in = jnp.where(filled[:, None], gathered, jnp.zeros_like(gathered))
        slot_mix = jnp.where(filled, flat_mix[route_ids], jnp.zeros((), jnp.float32))
        rows_cot = (slot_mix[:, None] * cotangent[token_ids].astype(jnp.float32)).astype(jnp.bfloat16)
        gate_mat = gate_weight[slot]
        up_mat = up_weight[slot]
        down_mat = down_weight[slot]
        gate_pre = jnp.dot(rows_in, gate_mat, preferred_element_type=jnp.float32)
        up_pre = jnp.dot(rows_in, up_mat, preferred_element_type=jnp.float32)
        sigma_gate = jax.nn.sigmoid(gate_pre)
        silu_gate = gate_pre * sigma_gate
        hidden = (silu_gate * up_pre).astype(jnp.bfloat16)
        summed = jnp.zeros((rows_in.shape[0], D), jnp.float32)
        for piece in range(2):
            lower = piece * half_units
            partial_value = jnp.dot(hidden[:, lower:lower + half_units], down_mat[lower:lower + half_units], preferred_element_type=jnp.float32)
            summed = summed + rounded(partial_value)
        expert_out = rounded(summed)
        carry = carry.at[token_ids].add(slot_mix[:, None] * expert_out)
        down_grad = jnp.dot(hidden.T, rows_cot, preferred_element_type=jnp.float32).astype(jnp.bfloat16)
        hidden_cot = jnp.dot(rows_cot, down_mat.T, preferred_element_type=jnp.float32)
        slope = sigma_gate * (1.0 + gate_pre * (1.0 - sigma_gate))
        gate_cot = (hidden_cot * up_pre * slope).astype(jnp.bfloat16)
        up_cot = (hidden_cot * silu_gate).astype(jnp.bfloat16)
        gate_grad = jnp.dot(rows_in.T, gate_cot, preferred_element_type=jnp.float32).astype(jnp.bfloat16)
        up_grad = jnp.dot(rows_in.T, up_cot, preferred_element_type=jnp.float32).astype(jnp.bfloat16)
        return carry, (gate_grad, up_grad, down_grad)

    start = jnp.zeros((TOKENS, D), jnp.float32)
    total, grads = lax.scan(one_slot, start, jnp.arange(N_EXPERT, dtype=jnp.int32))
    return total.astype(jnp.bfloat16), grads[0], grads[1], grads[2]
```

```python
import functools

import jax
import jax.numpy as jnp
from jax import lax
from jax.experimental import pallas as pl
from jax.experimental.pallas import tpu as pltpu
from jax.sharding import PartitionSpec as P


AXES = ("dp", "expert")
CORES = 2
SIDE = 2
F32 = jnp.float32
BF16 = jnp.bfloat16


def exchange_plan(tokens, cotangent, routes, gate_probs, matching, gate_weight, up_weight, down_weight):
    expert_count = lax.axis_size("expert")
    token_count, fan_out = routes.shape
    capacity = max(2, token_count * fan_out * 9 // (8 * expert_count))
    route_count = token_count * fan_out
    mix_weights = gate_probs / jnp.sum(gate_probs, axis=1, keepdims=True)
    flat_routes = routes.reshape(-1)
    expert_hit = flat_routes[:, None] == jnp.arange(matching.shape[0], dtype=jnp.int32)[None, :]
    host_of = jnp.sum(jnp.where(expert_hit, matching[None, :], 0), axis=1)
    host_hit = (host_of[:, None] == jnp.arange(expert_count, dtype=jnp.int32)[None, :]).astype(
        jnp.int32
    )
    running = jnp.cumsum(host_hit, axis=0)
    slot_rank = jnp.sum((running - 1) * host_hit, axis=1)
    position = host_of * capacity + slot_rank
    slot_table = (
        jnp.full((expert_count * capacity,), route_count, jnp.int32)
        .at[position]
        .set(jnp.arange(route_count, dtype=jnp.int32))
    )
    filled = slot_table < route_count
    route_ids = jnp.minimum(slot_table, route_count - 1)
    token_ids = jnp.where(filled, route_ids // fan_out, token_count)
    clamped_ids = route_ids // fan_out
    slot_mix = jnp.where(filled, jnp.take(mix_weights.reshape(-1), route_ids), 0.0)
    recv_rows = lax.all_to_all(
        jnp.take(tokens, token_ids, axis=0, mode="fill", fill_value=0),
        "expert",
        split_axis=0,
        concat_axis=0,
        tiled=True,
    )
    gathered = jnp.take(cotangent, clamped_ids, axis=0)
    recv_cot = lax.all_to_all(
        (slot_mix[:, None] * gathered.astype(jnp.float32)).astype(jnp.bfloat16),
        "expert",
        split_axis=0,
        concat_axis=0,
        tiled=True,
    )
    inputs, out_cot = (
        lax.all_gather(recv_rows, "dp", axis=1, tiled=True),
        lax.all_gather(recv_cot, "dp", axis=1, tiled=True),
    )
    gate_pre = jnp.dot(inputs, gate_weight[0], preferred_element_type=jnp.float32)
    up_pre = jnp.dot(inputs, up_weight[0], preferred_element_type=jnp.float32)
    sigma_gate = jax.nn.sigmoid(gate_pre)
    silu_gate = gate_pre * sigma_gate
    hidden = (silu_gate * up_pre).astype(jnp.bfloat16)
    partial_out = jnp.dot(hidden, down_weight[0], preferred_element_type=jnp.float32)
    contract_rows = (((0,), (0,)), ((), ()))
    down_grad = lax.dot_general(
        hidden, out_cot, contract_rows, preferred_element_type=jnp.float32
    ).astype(jnp.bfloat16)
    hidden_cot = lax.dot_general(
        out_cot, down_weight[0], (((1,), (1,)), ((), ())), preferred_element_type=jnp.float32
    )
    slope = sigma_gate * (1.0 + gate_pre * (1.0 - sigma_gate))
    gate_cot = (hidden_cot * up_pre * slope).astype(jnp.bfloat16)
    up_cot = (hidden_cot * silu_gate).astype(jnp.bfloat16)
    gate_grad = lax.dot_general(
        inputs, gate_cot, contract_rows, preferred_element_type=jnp.float32
    ).astype(jnp.bfloat16)
    up_grad = lax.dot_general(
        inputs, up_cot, contract_rows, preferred_element_type=jnp.float32
    ).astype(jnp.bfloat16)
    summed = lax.psum_scatter(
        partial_out.astype(jnp.bfloat16), "dp", scatter_dimension=1, tiled=True
    )
    merged = lax.all_to_all(summed, "expert", split_axis=0, concat_axis=0, tiled=True)
    half_width = merged.shape[1]
    expert_out = jnp.take(merged, position, axis=0).reshape(token_count, fan_out, half_width)
    layer_out = jnp.sum(mix_weights[:, :, None] * expert_out.astype(jnp.float32), axis=1).astype(
        jnp.bfloat16
    )
    return (layer_out, gate_grad[None], up_grad[None], down_grad[None])


def moves(expert_count):
    depth = expert_count // (SIDE * CORES)

    def table(step):
        pairs = []
        for y in range(2):
            for z in range(depth):
                for x in range(SIDE):
                    for core in range(CORES):
                        ty, tz, tx, tcore = step(y, z, x, core)
                        pairs.append(
                            (
                                y * expert_count + (z * SIDE + x) * CORES + core,
                                ty * expert_count + (tz * SIDE + tx) * CORES + tcore,
                            )
                        )
        return pairs

    shift = {
        by: table(lambda y, z, x, core, by=by: (y, (z + by) % depth, x, core))
        for by in range(1 - depth, depth)
        if by
    }
    swap = table(lambda y, z, x, core: (y, z, x, 1 - core))
    first = table(lambda y, z, x, core: (y, z, 1 - x, core) if core == 0 else (1 - y, z, x, core))
    second = table(lambda y, z, x, core: (1 - y, z, x, core) if core == 0 else (y, z, 1 - x, core))
    return depth, shift, swap, first, second


def dot(a, b):
    return jnp.dot(a, b, preferred_element_type=F32)


def dot_rows(a, b):
    return lax.dot_general(a, b, (((0,), (0,)), ((), ())), preferred_element_type=F32)


def place(across, other, core):
    if across and other:
        return 3
    if across:
        return 1 + core
    if other:
        return 2 - core
    return 0


def row_weights(mix_ref, z, x, core, depth):
    block = (z * SIDE + x) * CORES + core
    lanes = lax.broadcasted_iota(jnp.int32, mix_ref.shape, 1)
    return jnp.sum(jnp.where(lanes == block, mix_ref[...], 0.0), axis=1, keepdims=True)


def rows_of(mine_ref, theirs_ref, other, core):
    return jnp.concatenate(
        [
            mine_ref[place(0, other, core)],
            mine_ref[place(1, other, core)],
            theirs_ref[place(0, other, 1 - core)],
            theirs_ref[place(1, other, 1 - core)],
        ],
        axis=0,
    )


def weights_of(mix_ref, where_ref, back, depth):
    z, x, core = lax.rem(where_ref[1] + depth - back, depth), where_ref[2], where_ref[3]
    return jnp.concatenate(
        [
            row_weights(mix_ref, z, x, core, depth),
            row_weights(mix_ref, z, 1 - x, core, depth),
            row_weights(mix_ref, z, x, 1 - core, depth),
            row_weights(mix_ref, z, 1 - x, 1 - core, depth),
        ],
        axis=0,
    )


def forward_kernel(back, depth, where_ref, mine_ref, theirs_ref, mix_ref, in_ref, down_ref, keep_ref, send_ref, pre_ref):
    y, core = where_ref[0], where_ref[3]
    width = pre_ref.shape[1] // 2
    half = mine_ref.shape[2]
    rows = mine_ref.shape[1]
    pre = dot(rows_of(mine_ref, theirs_ref, 0, core), in_ref[y])
    pre += dot(rows_of(mine_ref, theirs_ref, 1, core), in_ref[1 - y])
    pre_ref[...] = pre
    gate = pre[:, :width]
    hidden = (gate * jax.nn.sigmoid(gate) * pre[:, width:]).astype(BF16)
    weights = weights_of(mix_ref, where_ref, back, depth)
    for other in range(2):
        side = y if other == 0 else 1 - y
        out = dot(hidden, down_ref[:, pl.ds(pl.multiple_of(side * half, half), half)])
        out = (weights * out).astype(BF16)
        keep_ref[place(0, other, core)] = out[:rows]
        keep_ref[place(1, other, core)] = out[rows : 2 * rows]
        send_ref[place(0, other, 1 - core)] = out[2 * rows : 3 * rows]
        send_ref[place(1, other, 1 - core)] = out[3 * rows :]


def forward(back, depth, where, mine, theirs, mix, in_weight, down):
    pieces, rows, half = mine.shape
    width = in_weight.shape[2]
    total = 4 * rows
    vmem = pl.BlockSpec(memory_space=pltpu.VMEM)
    return pl.pallas_call(
        functools.partial(forward_kernel, back, depth),
        out_shape=(
            jax.ShapeDtypeStruct(mine.shape, BF16),
            jax.ShapeDtypeStruct(mine.shape, BF16),
            jax.ShapeDtypeStruct((total, width), F32),
        ),
        in_specs=[pl.BlockSpec(memory_space=pltpu.SMEM)] + [vmem] * 5,
        out_specs=(vmem,) * 3,
        cost_estimate=pl.CostEstimate(
            flops=2 * total * half * width * 3, bytes_accessed=8 * mine.size, transcendentals=total * width // 2
        ),
    )(where, mine, theirs, mix, in_weight, down)


def backward_kernel(depth, where_ref, *refs):
    tokens = refs[: 2 * depth]
    cots = refs[2 * depth : 4 * depth]
    pres = refs[4 * depth : 5 * depth]
    mix_ref, down_ref, gate_out, up_out, down_out = refs[5 * depth : 5 * depth + 5]
    tok_buf, cot_buf, pre_buf, in_acc, down_acc, sems = refs[5 * depth + 5 :]
    step = pl.program_id(0)
    y, core = where_ref[0], where_ref[3]
    slot = lax.rem(step, 2)
    width = pre_buf.shape[2] // 2
    half = down_ref.shape[1] // 2

    def copies(group, to):
        return [
            pltpu.make_async_copy(tokens[group], tok_buf.at[to, 0], sems.at[to, 0]),
            pltpu.make_async_copy(tokens[depth + group], tok_buf.at[to, 1], sems.at[to, 1]),
            pltpu.make_async_copy(cots[group], cot_buf.at[to, 0], sems.at[to, 2]),
            pltpu.make_async_copy(cots[depth + group], cot_buf.at[to, 1], sems.at[to, 3]),
            pltpu.make_async_copy(pres[group], pre_buf.at[to], sems.at[to, 4]),
        ]

    @pl.when(step == 0)
    def _():
        for copy in copies(0, 0):
            copy.start()
        in_acc[...] = jnp.zeros_like(in_acc)
        down_acc[...] = jnp.zeros_like(down_acc)

    for group in range(1, depth):

        @pl.when(step + 1 == group)
        def _():
            for copy in copies(group, group % 2):
                copy.start()

    for copy in copies(0, slot):
        copy.wait()

    weights = weights_of(mix_ref, where_ref, step, depth)
    mine_cot, theirs_cot = cot_buf.at[slot, 0], cot_buf.at[slot, 1]
    near = (weights * rows_of(mine_cot, theirs_cot, 0, core).astype(F32)).astype(BF16)
    far = (weights * rows_of(mine_cot, theirs_cot, 1, core).astype(F32)).astype(BF16)
    near_at = pl.ds(pl.multiple_of(y * half, half), half)
    far_at = pl.ds(pl.multiple_of((1 - y) * half, half), half)
    contract = (((1,), (1,)), ((), ()))
    hidden_cot = lax.dot_general(near, down_ref[:, near_at], contract, preferred_element_type=F32)
    hidden_cot += lax.dot_general(far, down_ref[:, far_at], contract, preferred_element_type=F32)
    pre = pre_buf[slot]
    gate, up = pre[:, :width], pre[:, width:]
    sigma = jax.nn.sigmoid(gate)
    silu = gate * sigma
    hidden = (silu * up).astype(BF16)
    slope = sigma * (1.0 + gate * (1.0 - sigma))
    gate_cot = (hidden_cot * up * slope).astype(BF16)
    up_cot = (hidden_cot * silu).astype(BF16)
    both = jnp.concatenate([gate_cot, up_cot], axis=1)
    down_acc[0] += dot_rows(hidden, near)
    down_acc[1] += dot_rows(hidden, far)
    mine_tok, theirs_tok = tok_buf.at[slot, 0], tok_buf.at[slot, 1]
    in_acc[0] += dot_rows(rows_of(mine_tok, theirs_tok, 0, core), both)
    in_acc[1] += dot_rows(rows_of(mine_tok, theirs_tok, 1, core), both)

    @pl.when(step == depth - 1)
    def _():
        for other in range(2):
            side = y if other == 0 else 1 - y
            gate_out[side] = in_acc[other, :, :width].astype(BF16)
            up_out[side] = in_acc[other, :, width:].astype(BF16)
            down_out[:, pl.ds(pl.multiple_of(side * half, half), half)] = down_acc[other].astype(BF16)


def backward(depth, where, tok_mine, tok_theirs, cot_mine, cot_theirs, pres, mix, down):
    pieces, rows, half = tok_mine[0].shape
    total, width = pres[0].shape
    units = width // 2
    vmem = pl.BlockSpec(memory_space=pltpu.VMEM)
    hbm = pl.BlockSpec(memory_space=pl.ANY)
    return pl.pallas_call(
        functools.partial(backward_kernel, depth),
        grid=(depth,),
        out_shape=(
            jax.ShapeDtypeStruct((2, half, units), BF16),
            jax.ShapeDtypeStruct((2, half, units), BF16),
            jax.ShapeDtypeStruct((units, 2 * half), BF16),
        ),
        in_specs=[pl.BlockSpec(memory_space=pltpu.SMEM)] + [hbm] * (5 * depth) + [vmem] * 2,
        out_specs=(vmem,) * 3,
        scratch_shapes=[
            pltpu.VMEM((2, 2, pieces, rows, half), BF16),
            pltpu.VMEM((2, 2, pieces, rows, half), BF16),
            pltpu.VMEM((2, total, width), F32),
            pltpu.VMEM((2, half, width), F32),
            pltpu.VMEM((2, units, half), F32),
            pltpu.SemaphoreType.DMA((2, 5)),
        ],
        cost_estimate=pl.CostEstimate(
            flops=depth * 2 * total * half * width * 4,
            bytes_accessed=depth * 12 * total * half,
            transcendentals=depth * total * units,
        ),
    )(where, *tok_mine, *tok_theirs, *cot_mine, *cot_theirs, *pres, mix, down)


def gather_plan(tokens, cotangent, routes, gate_probs, matching, gate_weight, up_weight, down_weight):
    expert_count = lax.axis_size("expert")
    depth, shift, swap, first, second = moves(expert_count)

    def send(value, pairs):
        return lax.ppermute(value, AXES, pairs)

    rows, half = tokens.shape
    units = gate_weight.shape[2]
    y, at = lax.axis_index("dp"), lax.axis_index("expert")
    where = jnp.stack([y, at // (SIDE * CORES), (at // CORES) % SIDE, at % CORES]).astype(jnp.int32)

    along = [tokens]
    for _ in range(depth - 1):
        along.append(send(along[-1], shift[1]))
    tok_mine, tok_theirs = [], []
    for piece in along:
        a = send(piece, first)
        b = send(piece, second)
        d = send(a, second)
        stack = jnp.stack([piece, a, b, d])
        tok_mine.append(stack)
        tok_theirs.append(send(stack, swap))

    a = send(cotangent, first)
    b = send(cotangent, second)
    d = send(a, second)
    cot_mine = [jnp.stack([cotangent, a, b, d])]
    for _ in range(depth - 1):
        cot_mine.append(send(cot_mine[-1], shift[1]))
    cot_theirs = [send(stack, swap) for stack in cot_mine]

    mix = gate_probs / jnp.sum(gate_probs, axis=1, keepdims=True)
    hit = routes[:, :, None] == jnp.arange(matching.shape[0], dtype=jnp.int32)
    host = jnp.sum(jnp.where(hit, matching, 0), axis=2)
    slots = jnp.arange(expert_count, dtype=jnp.int32)
    per_slot = jnp.sum(jnp.where(host[None] == slots[:, None, None], mix[None], 0.0), axis=2)
    mix = lax.all_to_all(per_slot, "expert", split_axis=0, concat_axis=0, tiled=True).T

    in_weight = jnp.concatenate([gate_weight[0], up_weight[0]], axis=1).reshape(2, half, 2 * units)
    down = down_weight[0]

    pres, out = [], None
    for back in range(depth):
        keep, give, pre = forward(
            back, depth, where, tok_mine[back], tok_theirs[back], mix, in_weight, down
        )
        pres.append(pre)
        got = send(give, swap)
        d = send((keep[3].astype(F32) + got[3]).astype(BF16), second)
        a = send((keep[1].astype(F32) + got[1] + d).astype(BF16), first)
        b = send((keep[2].astype(F32) + got[2]).astype(BF16), second)
        own = keep[0].astype(F32) + got[0] + a + b
        if back:
            own = send(own.astype(BF16), shift[-back]).astype(F32)
        out = own if out is None else out + own

    gate_grad, up_grad, down_grad = backward(
        depth, where, tok_mine, tok_theirs, cot_mine, cot_theirs, pres, mix, down
    )
    return (
        out.astype(BF16),
        gate_grad.reshape(1, 2 * half, units),
        up_grad.reshape(1, 2 * half, units),
        down_grad[None],
    )


def solution(mesh):
    experts = mesh.shape["expert"]
    square = mesh.shape["dp"] == 2 and experts % (SIDE * CORES) == 0

    def on_device(*args):
        dense = 2 * args[2].shape[1] >= experts
        return gather_plan(*args) if square and dense else exchange_plan(*args)

    placed = (
        P("expert", "dp"),
        P("expert", "dp"),
        P("expert", None),
        P("expert", None),
        P(),
        P("expert", None, "dp"),
        P("expert", None, "dp"),
        P("expert", "dp", None),
    )
    return jax.shard_map(
        on_device,
        mesh=mesh,
        in_specs=placed,
        out_specs=(
            P("expert", "dp"),
            P("expert", None, "dp"),
            P("expert", None, "dp"),
            P("expert", "dp", None),
        ),
        check_vma=False,
    )
```

```python
import functools

import jax
import jax.numpy as jnp
from jax import lax
from jax.experimental import pallas as pl
from jax.experimental.pallas import tpu as pltpu
from jax.sharding import PartitionSpec as P


AXES = ("dp", "expert")
CORES = 2
SIDE = 2
F32 = jnp.float32
BF16 = jnp.bfloat16


def exchange_plan(tokens, cotangent, routes, gate_probs, matching, gate_weight, up_weight, down_weight):
    expert_count = lax.axis_size("expert")
    token_count, fan_out = routes.shape
    capacity = max(2, token_count * fan_out * 9 // (8 * expert_count))
    route_count = token_count * fan_out
    mix_weights = gate_probs / jnp.sum(gate_probs, axis=1, keepdims=True)
    flat_routes = routes.reshape(-1)
    expert_hit = flat_routes[:, None] == jnp.arange(matching.shape[0], dtype=jnp.int32)[None, :]
    host_of = jnp.sum(jnp.where(expert_hit, matching[None, :], 0), axis=1)
    host_hit = (host_of[:, None] == jnp.arange(expert_count, dtype=jnp.int32)[None, :]).astype(
        jnp.int32
    )
    running = jnp.cumsum(host_hit, axis=0)
    slot_rank = jnp.sum((running - 1) * host_hit, axis=1)
    position = host_of * capacity + slot_rank
    slot_table = (
        jnp.full((expert_count * capacity,), route_count, jnp.int32)
        .at[position]
        .set(jnp.arange(route_count, dtype=jnp.int32))
    )
    filled = slot_table < route_count
    route_ids = jnp.minimum(slot_table, route_count - 1)
    token_ids = jnp.where(filled, route_ids // fan_out, token_count)
    clamped_ids = route_ids // fan_out
    slot_mix = jnp.where(filled, jnp.take(mix_weights.reshape(-1), route_ids), 0.0)
    recv_rows = lax.all_to_all(
        jnp.take(tokens, token_ids, axis=0, mode="fill", fill_value=0),
        "expert",
        split_axis=0,
        concat_axis=0,
        tiled=True,
    )
    gathered = jnp.take(cotangent, clamped_ids, axis=0)
    recv_cot = lax.all_to_all(
        (slot_mix[:, None] * gathered.astype(jnp.float32)).astype(jnp.bfloat16),
        "expert",
        split_axis=0,
        concat_axis=0,
        tiled=True,
    )
    inputs, out_cot = (
        lax.all_gather(recv_rows, "dp", axis=1, tiled=True),
        lax.all_gather(recv_cot, "dp", axis=1, tiled=True),
    )
    gate_pre = jnp.dot(inputs, gate_weight[0], preferred_element_type=jnp.float32)
    up_pre = jnp.dot(inputs, up_weight[0], preferred_element_type=jnp.float32)
    sigma_gate = jax.nn.sigmoid(gate_pre)
    silu_gate = gate_pre * sigma_gate
    hidden = (silu_gate * up_pre).astype(jnp.bfloat16)
    partial_out = jnp.dot(hidden, down_weight[0], preferred_element_type=jnp.float32)
    contract_rows = (((0,), (0,)), ((), ()))
    down_grad = lax.dot_general(
        hidden, out_cot, contract_rows, preferred_element_type=jnp.float32
    ).astype(jnp.bfloat16)
    hidden_cot = lax.dot_general(
        out_cot, down_weight[0], (((1,), (1,)), ((), ())), preferred_element_type=jnp.float32
    )
    slope = sigma_gate * (1.0 + gate_pre * (1.0 - sigma_gate))
    gate_cot = (hidden_cot * up_pre * slope).astype(jnp.bfloat16)
    up_cot = (hidden_cot * silu_gate).astype(jnp.bfloat16)
    gate_grad = lax.dot_general(
        inputs, gate_cot, contract_rows, preferred_element_type=jnp.float32
    ).astype(jnp.bfloat16)
    up_grad = lax.dot_general(
        inputs, up_cot, contract_rows, preferred_element_type=jnp.float32
    ).astype(jnp.bfloat16)
    summed = lax.psum_scatter(
        partial_out.astype(jnp.bfloat16), "dp", scatter_dimension=1, tiled=True
    )
    merged = lax.all_to_all(summed, "expert", split_axis=0, concat_axis=0, tiled=True)
    half_width = merged.shape[1]
    expert_out = jnp.take(merged, position, axis=0).reshape(token_count, fan_out, half_width)
    layer_out = jnp.sum(mix_weights[:, :, None] * expert_out.astype(jnp.float32), axis=1).astype(
        jnp.bfloat16
    )
    return (layer_out, gate_grad[None], up_grad[None], down_grad[None])


def moves(expert_count):
    depth = expert_count // (SIDE * CORES)

    def table(step):
        pairs = []
        for y in range(2):
            for z in range(depth):
                for x in range(SIDE):
                    for core in range(CORES):
                        ty, tz, tx, tcore = step(y, z, x, core)
                        pairs.append(
                            (
                                y * expert_count + (z * SIDE + x) * CORES + core,
                                ty * expert_count + (tz * SIDE + tx) * CORES + tcore,
                            )
                        )
        return pairs

    shift = {
        by: table(lambda y, z, x, core, by=by: (y, (z + by) % depth, x, core))
        for by in range(1 - depth, depth)
        if by
    }
    swap = table(lambda y, z, x, core: (y, z, x, 1 - core))
    first = table(lambda y, z, x, core: (y, z, 1 - x, core) if core == 0 else (1 - y, z, x, core))
    second = table(lambda y, z, x, core: (1 - y, z, x, core) if core == 0 else (y, z, 1 - x, core))
    return depth, shift, swap, first, second


def dot(a, b):
    return jnp.dot(a, b, preferred_element_type=F32)


def dot_rows(a, b):
    return lax.dot_general(a, b, (((0,), (0,)), ((), ())), preferred_element_type=F32)


def dot_columns(a, b):
    return lax.dot_general(a, b, (((1,), (1,)), ((), ())), preferred_element_type=F32)


def piece_windows(where_ref, rows, half):
    y, core = where_ref[0], where_ref[3]

    def window(lower, other):
        side = jnp.where(other == 1, 1 - y, y)
        return (
            pl.ds(pl.multiple_of(lower * rows, rows), rows),
            pl.ds(pl.multiple_of(side * half, half), half),
        )

    return window(0, 0), window(1 - core, core), window(core, 1 - core), window(1, 1)


def row_weights(mix_ref, where_ref, back, depth, slot):
    core = where_ref[3]
    z, x = lax.rem(where_ref[1] + depth - back, depth), where_ref[2]
    parity = core if slot == 0 else 1 - core
    lanes = lax.broadcasted_iota(jnp.int32, mix_ref.shape, 1)
    columns = []
    for across in (x, 1 - x):
        block = (z * SIDE + across) * CORES + core
        hit = lanes == block * CORES + parity
        columns.append(jnp.sum(jnp.where(hit, mix_ref[...], 0.0), axis=1, keepdims=True))
    return jnp.concatenate(columns, axis=0)


def forward_kernel(back, depth, fresh, where_ref, *refs):
    pieces, refs = refs[:4], refs[4:]
    mix_ref, ins, downs, refs = refs[0], refs[1:3], refs[3:5], refs[5 if fresh else 6 :]
    outs, pre_ref, all_ref, x_buf, o_buf, sem = refs[:4], refs[4], refs[5], refs[6], refs[7], refs[8]
    rows, half = pieces[0].shape
    windows = piece_windows(where_ref, rows, half)
    for window, piece in zip(windows, pieces):
        x_buf[window] = piece[...]
    keep = pltpu.make_async_copy(x_buf, all_ref.at[pl.ds(2 * rows * back, 2 * rows)], sem)
    keep.start()
    width = ins[0].shape[1]
    units = width // 2
    for slot in range(CORES):
        pre = dot(x_buf[...], ins[slot][...])
        pre_ref[:, slot * width : (slot + 1) * width] = pre
        gate = pre[:, :units]
        hidden = (gate * jax.nn.sigmoid(gate) * pre[:, units:]).astype(BF16)
        out = row_weights(mix_ref, where_ref, back, depth, slot) * dot(hidden, downs[slot][...])
        if slot == 0:
            o_buf[...] = out
        else:
            o_buf[...] += out
    for window, ref in zip(windows, outs):
        ref[...] = o_buf[window].astype(BF16)
    keep.wait()


def forward(back, depth, where, pieces, mix, ins, downs, rows_all):
    rows, half = pieces[0].shape
    width = ins[0].shape[1]
    total = 2 * rows
    fresh = rows_all is None
    vmem = pl.BlockSpec(memory_space=pltpu.VMEM)
    hbm = pl.BlockSpec(memory_space=pl.ANY)
    return pl.pallas_call(
        functools.partial(forward_kernel, back, depth, fresh),
        out_shape=tuple([jax.ShapeDtypeStruct((rows, half), BF16)] * 4)
        + (
            jax.ShapeDtypeStruct((total, CORES * width), F32),
            jax.ShapeDtypeStruct((depth * total, 2 * half), BF16),
        ),
        in_specs=[pl.BlockSpec(memory_space=pltpu.SMEM)] + [vmem] * 9 + ([] if fresh else [hbm]),
        out_specs=(vmem,) * 5 + (hbm,),
        input_output_aliases={} if fresh else {10: 5},
        scratch_shapes=[
            pltpu.VMEM((total, 2 * half), BF16),
            pltpu.VMEM((total, 2 * half), F32),
            pltpu.SemaphoreType.DMA,
        ],
        compiler_params=pltpu.CompilerParams(vmem_limit_bytes=14 << 20),
        cost_estimate=pl.CostEstimate(
            flops=2 * total * half * width * 6, bytes_accessed=12 * total * half, transcendentals=total * width
        ),
    )(where, *pieces, mix, *ins, *downs, *([] if fresh else [rows_all]))


def backward_kernel(back, depth, fresh, where_ref, *refs):
    pair_ref, far_ref, pre_ref, mix_ref = refs[:4]
    downs, refs = refs[4:6], refs[6 if fresh else 9 :]
    cot_all, hid_all, pre_all, c_buf, w_buf, h_buf, g_buf, sems = refs
    rows, half = pair_ref.shape[1:]
    total = 2 * rows
    windows = piece_windows(where_ref, rows, half)
    for window, piece in zip(windows, (pair_ref.at[0], pair_ref.at[1], far_ref.at[0], far_ref.at[1])):
        c_buf[window] = piece[...]
    width = pre_ref.shape[1] // 2
    units = width // 2
    at = pl.ds(total * back, total)
    copies = []
    for slot in range(CORES):
        weights = row_weights(mix_ref, where_ref, back, depth, slot)
        cot = (weights * c_buf[...].astype(F32)).astype(BF16)
        w_buf[slot] = cot
        hidden_cot = dot_columns(cot, downs[slot][...])
        gate = pre_ref[:, slot * width : slot * width + units]
        up = pre_ref[:, slot * width + units : (slot + 1) * width]
        sigma = jax.nn.sigmoid(gate)
        silu = gate * sigma
        h_buf[slot] = (silu * up).astype(BF16)
        slope = sigma * (1.0 + gate * (1.0 - sigma))
        g_buf[slot, :, :units] = (hidden_cot * up * slope).astype(BF16)
        g_buf[slot, :, units:] = (hidden_cot * silu).astype(BF16)
        for number, (buf, to) in enumerate(((w_buf, cot_all), (h_buf, hid_all), (g_buf, pre_all))):
            copies.append(pltpu.make_async_copy(buf.at[slot], to.at[slot, at], sems.at[slot, number]))
            copies[-1].start()
    for copy in copies:
        copy.wait()


def backward(back, depth, where, pair, far, pre, mix, downs, kept):
    rows, half = pair.shape[1:]
    width = pre.shape[1] // 2
    total = 2 * rows
    fresh = kept is None
    vmem = pl.BlockSpec(memory_space=pltpu.VMEM)
    hbm = pl.BlockSpec(memory_space=pl.ANY)
    return pl.pallas_call(
        functools.partial(backward_kernel, back, depth, fresh),
        out_shape=tuple(
            jax.ShapeDtypeStruct((CORES, depth * total, columns), BF16)
            for columns in (2 * half, width // 2, width)
        ),
        in_specs=[pl.BlockSpec(memory_space=pltpu.SMEM)] + [vmem] * 6 + ([] if fresh else [hbm] * 3),
        out_specs=(hbm,) * 3,
        input_output_aliases={} if fresh else {7: 0, 8: 1, 9: 2},
        scratch_shapes=[
            pltpu.VMEM((total, 2 * half), BF16),
            pltpu.VMEM((CORES, total, 2 * half), BF16),
            pltpu.VMEM((CORES, total, width // 2), BF16),
            pltpu.VMEM((CORES, total, width), BF16),
            pltpu.SemaphoreType.DMA((CORES, 3)),
        ],
        compiler_params=pltpu.CompilerParams(vmem_limit_bytes=16 << 20),
        cost_estimate=pl.CostEstimate(
            flops=2 * total * half * width * 2, bytes_accessed=20 * total * half, transcendentals=total * width
        ),
    )(where, pair, far, pre, mix, *downs, *([] if fresh else kept))


def partner_grads_kernel(rows_ref, cot_ref, hid_ref, pre_ref, in_ref, down_ref):
    in_ref[...] = dot_rows(rows_ref[...], pre_ref[0]).astype(BF16)
    down_ref[...] = dot_rows(hid_ref[0], cot_ref[0]).astype(BF16)


def own_grads_kernel(rows_ref, cot_ref, hid_ref, pre_ref, in_got, down_got, gate_ref, up_ref, down_ref):
    units = gate_ref.shape[1]
    grads = dot_rows(rows_ref[...], pre_ref[0]) + in_got[...].astype(F32)
    gate_ref[...] = grads[:, :units].astype(BF16)
    up_ref[...] = grads[:, units:].astype(BF16)
    down_ref[...] = (dot_rows(hid_ref[0], cot_ref[0]) + down_got[...].astype(F32)).astype(BF16)


def weight_grads(slot, rows_all, kept, got):
    cot_all, hid_all, pre_all = kept
    total, features = rows_all.shape
    units, width = hid_all.shape[2], pre_all.shape[2]
    tile = min(256, features)
    steps = features // tile

    def tall(columns):
        return pl.BlockSpec((tile, columns), lambda i: (i, 0))

    flat = pl.BlockSpec((units, tile), lambda i: (0, i))
    in_specs = [
        pl.BlockSpec((total, tile), lambda i: (0, i)),
        pl.BlockSpec((1, total, tile), lambda i: (slot, 0, i)),
        pl.BlockSpec((1, total, units), lambda i: (slot, 0, 0)),
        pl.BlockSpec((1, total, width), lambda i: (slot, 0, 0)),
    ]
    shapes = {
        "in": jax.ShapeDtypeStruct((features, width), BF16),
        "half": jax.ShapeDtypeStruct((features, units), BF16),
        "down": jax.ShapeDtypeStruct((units, features), BF16),
    }
    params = dict(
        grid=(steps,),
        compiler_params=pltpu.CompilerParams(vmem_limit_bytes=24 << 20),
        cost_estimate=pl.CostEstimate(
            flops=2 * total * features * (width + units),
            bytes_accessed=2 * (2 * total * features + features * width * 3),
            transcendentals=0,
        ),
    )
    if got is None:
        return pl.pallas_call(
            partner_grads_kernel,
            out_shape=(shapes["in"], shapes["down"]),
            in_specs=in_specs,
            out_specs=(tall(width), flat),
            **params,
        )(rows_all, cot_all, hid_all, pre_all)
    return pl.pallas_call(
        own_grads_kernel,
        out_shape=(shapes["half"], shapes["half"], shapes["down"]),
        in_specs=in_specs + [tall(width), flat],
        out_specs=(tall(units), tall(units), flat),
        **params,
    )(rows_all, cot_all, hid_all, pre_all, *got)


def gather_plan(tokens, cotangent, routes, gate_probs, matching, gate_weight, up_weight, down_weight):
    expert_count = lax.axis_size("expert")
    depth, shift, swap, first, second = moves(expert_count)

    def send(value, pairs):
        return lax.ppermute(value, AXES, pairs)

    y, at = lax.axis_index("dp"), lax.axis_index("expert")
    where = jnp.stack([y, at // (SIDE * CORES), (at // CORES) % SIDE, at % CORES]).astype(jnp.int32)

    down = down_weight[0]
    downs = (down, send(down, swap))
    in_weight = jnp.concatenate([gate_weight[0], up_weight[0]], axis=1)
    ins = (in_weight, send(in_weight, swap))

    along = [tokens]
    for _ in range(1, depth):
        along.append(send(along[-1], shift[1]))
    pieces = []
    for piece in along:
        a = send(piece, first)
        b = send(piece, second)
        d = send(a, second)
        pieces.append((piece, a, b, d))

    pairs = [jnp.stack([cotangent, send(cotangent, first)])]
    for _ in range(1, depth):
        pairs.append(send(pairs[-1], shift[1]))
    fars = [send(pair, second) for pair in pairs]

    mix = gate_probs / jnp.sum(gate_probs, axis=1, keepdims=True)
    hit = routes[:, :, None] == jnp.arange(matching.shape[0], dtype=jnp.int32)
    host = jnp.sum(jnp.where(hit, matching, 0), axis=2)
    slots = jnp.arange(expert_count, dtype=jnp.int32)
    slots = (slots[:, None] // CORES * CORES + jnp.arange(CORES, dtype=jnp.int32)).reshape(-1)
    per_slot = jnp.sum(jnp.where(host[None] == slots[:, None, None], mix[None], 0.0), axis=2)
    mix = lax.all_to_all(per_slot, "expert", split_axis=0, concat_axis=0, tiled=True).T

    rows_all, pres, out = None, [], None
    for back in range(depth):
        *got, pre, rows_all = forward(back, depth, where, pieces[back], mix, ins, downs, rows_all)
        pres.append(pre)
        own, a, b, d = got
        d = send(d, second)
        b = send(b, second)
        a = (a.astype(F32) + d).astype(BF16)
        a = send(a, first)
        own = own.astype(F32) + a + b
        if back:
            own = send(own.astype(BF16), shift[-back]).astype(F32)
        out = own if out is None else out + own

    kept = None
    for back in range(depth):
        kept = backward(back, depth, where, pairs[back], fars[back], pres[back], mix, downs, kept)
    in_part, down_part = weight_grads(1, rows_all, kept, None)
    got = (send(in_part, swap), send(down_part, swap))
    gate_grad, up_grad, down_grad = weight_grads(0, rows_all, kept, got)
    return out.astype(BF16), gate_grad[None], up_grad[None], down_grad[None]


def solution(mesh):
    experts = mesh.shape["expert"]
    square = mesh.shape["dp"] == 2 and experts % (SIDE * CORES) == 0

    def on_device(*args):
        dense = 2 * args[2].shape[1] >= experts
        if not (square and dense):
            return exchange_plan(*args)
        return gather_plan(*args)

    placed = (
        P("expert", "dp"),
        P("expert", "dp"),
        P("expert", None),
        P("expert", None),
        P(),
        P("expert", None, "dp"),
        P("expert", None, "dp"),
        P("expert", "dp", None),
    )
    return jax.shard_map(
        on_device,
        mesh=mesh,
        in_specs=placed,
        out_specs=(
            P("expert", "dp"),
            P("expert", None, "dp"),
            P("expert", None, "dp"),
            P("expert", "dp", None),
        ),
        check_vma=False,
    )
```

```python
import functools

import jax
import jax.numpy as jnp
from jax import lax
from jax.experimental import pallas as pl
from jax.experimental.pallas import tpu as pltpu
from jax.sharding import PartitionSpec as P


AXES = ("dp", "expert")
CORES = 2
SIDE = 2
GROUP = 2
TILE = 512
F32 = jnp.float32
BF16 = jnp.bfloat16


def exchange_plan(tokens, cotangent, routes, gate_probs, matching, gate_weight, up_weight, down_weight):
    expert_count = lax.axis_size("expert")
    token_count, fan_out = routes.shape
    capacity = max(2, token_count * fan_out * 9 // (8 * expert_count))
    route_count = token_count * fan_out
    mix_weights = gate_probs / jnp.sum(gate_probs, axis=1, keepdims=True)
    flat_routes = routes.reshape(-1)
    expert_hit = flat_routes[:, None] == jnp.arange(matching.shape[0], dtype=jnp.int32)[None, :]
    host_of = jnp.sum(jnp.where(expert_hit, matching[None, :], 0), axis=1)
    host_hit = (host_of[:, None] == jnp.arange(expert_count, dtype=jnp.int32)[None, :]).astype(
        jnp.int32
    )
    running = jnp.cumsum(host_hit, axis=0)
    slot_rank = jnp.sum((running - 1) * host_hit, axis=1)
    position = host_of * capacity + slot_rank
    slot_table = (
        jnp.full((expert_count * capacity,), route_count, jnp.int32)
        .at[position]
        .set(jnp.arange(route_count, dtype=jnp.int32))
    )
    filled = slot_table < route_count
    route_ids = jnp.minimum(slot_table, route_count - 1)
    token_ids = jnp.where(filled, route_ids // fan_out, token_count)
    clamped_ids = route_ids // fan_out
    slot_mix = jnp.where(filled, jnp.take(mix_weights.reshape(-1), route_ids), 0.0)
    recv_rows = lax.all_to_all(
        jnp.take(tokens, token_ids, axis=0, mode="fill", fill_value=0),
        "expert",
        split_axis=0,
        concat_axis=0,
        tiled=True,
    )
    gathered = jnp.take(cotangent, clamped_ids, axis=0)
    recv_cot = lax.all_to_all(
        (slot_mix[:, None] * gathered.astype(jnp.float32)).astype(jnp.bfloat16),
        "expert",
        split_axis=0,
        concat_axis=0,
        tiled=True,
    )
    inputs, out_cot = (
        lax.all_gather(recv_rows, "dp", axis=1, tiled=True),
        lax.all_gather(recv_cot, "dp", axis=1, tiled=True),
    )
    gate_pre = jnp.dot(inputs, gate_weight[0], preferred_element_type=jnp.float32)
    up_pre = jnp.dot(inputs, up_weight[0], preferred_element_type=jnp.float32)
    sigma_gate = jax.nn.sigmoid(gate_pre)
    silu_gate = gate_pre * sigma_gate
    hidden = (silu_gate * up_pre).astype(jnp.bfloat16)
    partial_out = jnp.dot(hidden, down_weight[0], preferred_element_type=jnp.float32)
    contract_rows = (((0,), (0,)), ((), ()))
    down_grad = lax.dot_general(
        hidden, out_cot, contract_rows, preferred_element_type=jnp.float32
    ).astype(jnp.bfloat16)
    hidden_cot = lax.dot_general(
        out_cot, down_weight[0], (((1,), (1,)), ((), ())), preferred_element_type=jnp.float32
    )
    slope = sigma_gate * (1.0 + gate_pre * (1.0 - sigma_gate))
    gate_cot = (hidden_cot * up_pre * slope).astype(jnp.bfloat16)
    up_cot = (hidden_cot * silu_gate).astype(jnp.bfloat16)
    gate_grad = lax.dot_general(
        inputs, gate_cot, contract_rows, preferred_element_type=jnp.float32
    ).astype(jnp.bfloat16)
    up_grad = lax.dot_general(
        inputs, up_cot, contract_rows, preferred_element_type=jnp.float32
    ).astype(jnp.bfloat16)
    summed = lax.psum_scatter(
        partial_out.astype(jnp.bfloat16), "dp", scatter_dimension=1, tiled=True
    )
    merged = lax.all_to_all(summed, "expert", split_axis=0, concat_axis=0, tiled=True)
    half_width = merged.shape[1]
    expert_out = jnp.take(merged, position, axis=0).reshape(token_count, fan_out, half_width)
    layer_out = jnp.sum(mix_weights[:, :, None] * expert_out.astype(jnp.float32), axis=1).astype(
        jnp.bfloat16
    )
    return (layer_out, gate_grad[None], up_grad[None], down_grad[None])


def moves(expert_count):
    depth = expert_count // (SIDE * CORES)

    def table(step):
        pairs = []
        for y in range(2):
            for z in range(depth):
                for x in range(SIDE):
                    for core in range(CORES):
                        ty, tz, tx, tcore = step(y, z, x, core)
                        pairs.append(
                            (
                                y * expert_count + (z * SIDE + x) * CORES + core,
                                ty * expert_count + (tz * SIDE + tx) * CORES + tcore,
                            )
                        )
        return pairs

    shift = {
        by: table(lambda y, z, x, core, by=by: (y, (z + by) % depth, x, core))
        for by in range(1 - depth, depth)
        if by
    }
    swap = table(lambda y, z, x, core: (y, z, x, 1 - core))
    first = table(lambda y, z, x, core: (y, z, 1 - x, core) if core == 0 else (1 - y, z, x, core))
    second = table(lambda y, z, x, core: (1 - y, z, x, core) if core == 0 else (y, z, 1 - x, core))
    return depth, shift, swap, first, second


def dot(a, b):
    return jnp.dot(a, b, preferred_element_type=F32)


def dot_rows(a, b):
    return lax.dot_general(a, b, (((0,), (0,)), ((), ())), preferred_element_type=F32)


def dot_columns(a, b):
    return lax.dot_general(a, b, (((1,), (1,)), ((), ())), preferred_element_type=F32)


def piece_windows(where_ref, member, rows, half):
    y, core = where_ref[0], where_ref[3]

    def window(lower, other):
        side = jnp.where(other == 1, 1 - y, y)
        return (
            pl.ds(pl.multiple_of((2 * member + lower) * rows, rows), rows),
            pl.ds(pl.multiple_of(side * half, half), half),
        )

    return window(0, 0), window(1 - core, core), window(core, 1 - core), window(1, 1)


def row_weights(mix_ref, where_ref, backs, depth, slot):
    core, x = where_ref[3], where_ref[2]
    parity = core if slot == 0 else 1 - core
    lanes = lax.broadcasted_iota(jnp.int32, mix_ref.shape, 1)
    columns = []
    for back in backs:
        z = lax.rem(where_ref[1] + depth - back, depth)
        for across in (x, 1 - x):
            block = (z * SIDE + across) * CORES + core
            hit = lanes == block * CORES + parity
            columns.append(jnp.sum(jnp.where(hit, mix_ref[...], 0.0), axis=1, keepdims=True))
    return jnp.concatenate(columns, axis=0)


def forward_kernel(backs, depth, sets, fresh, where_ref, *refs):
    pieces, refs = refs[: 4 * sets], refs[4 * sets :]
    mix_ref, ins, downs, refs = refs[0], refs[1:3], refs[3:5], refs[5 if fresh else 6 :]
    outs, pre_ref, all_ref, x_buf, o_buf, sem = refs[:4], refs[4], refs[5], refs[6], refs[7], refs[8]
    rows, half = pieces[0].shape[1:]
    member = 0
    for number in range(sets):
        group = pieces[4 * number : 4 * number + 4]
        for inner in range(group[0].shape[0]):
            for window, piece in zip(piece_windows(where_ref, member, rows, half), group):
                x_buf[window] = piece[inner]
            member += 1
    total = 2 * rows * len(backs)
    keep = pltpu.make_async_copy(x_buf, all_ref.at[pl.ds(2 * rows * backs[0], total)], sem)
    keep.start()
    width = ins[0].shape[1]
    units = width // 2
    cut = width * 2 // 3
    for slot in range(CORES):
        pre_ref[:, slot * width : slot * width + cut] = dot(x_buf[...], ins[slot][:, :cut])
    last = dot(x_buf[...], jnp.concatenate([ins[0][:, cut:], ins[1][:, cut:]], axis=1))
    pre_ref[:, cut:width] = last[:, : width - cut]
    pre_ref[:, width + cut :] = last[:, width - cut :]
    hiddens = []
    for slot in range(CORES):
        gate = pre_ref[:, slot * width : slot * width + units]
        up = pre_ref[:, slot * width + units : (slot + 1) * width]
        weights = row_weights(mix_ref, where_ref, backs, depth, slot)
        hiddens.append((weights * (gate * jax.nn.sigmoid(gate) * up)).astype(BF16))
    o_buf[...] = dot(
        jnp.concatenate(hiddens, axis=1), jnp.concatenate([downs[0][...], downs[1][...]], axis=0)
    ).astype(BF16)
    for member in range(len(backs)):
        for window, ref in zip(piece_windows(where_ref, member, rows, half), outs):
            ref[member] = o_buf[window]
    keep.wait()


def forward(backs, depth, where, sets, mix, ins, downs, rows_all):
    rows, half = sets[0][0].shape[1:]
    width = ins[0].shape[1]
    total = 2 * rows * len(backs)
    fresh = rows_all is None
    flat = [piece for pieces in sets for piece in pieces]
    vmem = pl.BlockSpec(memory_space=pltpu.VMEM)
    hbm = pl.BlockSpec(memory_space=pl.ANY)
    return pl.pallas_call(
        functools.partial(forward_kernel, backs, depth, len(sets), fresh),
        out_shape=tuple([jax.ShapeDtypeStruct((len(backs), rows, half), BF16)] * 4)
        + (
            jax.ShapeDtypeStruct((total, CORES * width), F32),
            jax.ShapeDtypeStruct((depth * 2 * rows, 2 * half), BF16),
        ),
        in_specs=[pl.BlockSpec(memory_space=pltpu.SMEM)]
        + [vmem] * (len(flat) + 5)
        + ([] if fresh else [hbm]),
        out_specs=(vmem,) * 5 + (hbm,),
        input_output_aliases={} if fresh else {len(flat) + 6: 5},
        scratch_shapes=[
            pltpu.VMEM((total, 2 * half), BF16),
            pltpu.VMEM((total, 2 * half), BF16),
            pltpu.SemaphoreType.DMA,
        ],
        compiler_params=pltpu.CompilerParams(vmem_limit_bytes=20 << 20),
        cost_estimate=pl.CostEstimate(
            flops=2 * total * half * width * 6, bytes_accessed=12 * total * half, transcendentals=total * width
        ),
    )(where, *flat, mix, *ins, *downs, *([] if fresh else [rows_all]))


def backward_kernel(backs, depth, fresh, where_ref, *refs):
    count = len(backs)
    pairs, fars, refs = refs[:count], refs[count : 2 * count], refs[2 * count :]
    pre_ref, mix_ref, downs, refs = refs[0], refs[1], refs[2:4], refs[4 if fresh else 7 :]
    cot_all, hid_all, pre_all, c_buf, h_buf, g_buf, sems = refs
    rows, half = pairs[0].shape[1:]
    total = 2 * rows * count
    for member in range(count):
        pieces = (pairs[member].at[0], pairs[member].at[1], fars[member].at[0], fars[member].at[1])
        for window, piece in zip(piece_windows(where_ref, member, rows, half), pieces):
            c_buf[window] = piece[...]
    at = pl.ds(2 * rows * backs[0], total)
    copies = [pltpu.make_async_copy(c_buf, cot_all.at[at], sems.at[CORES, 0])]
    copies[0].start()
    width = pre_ref.shape[1] // 2
    units = width // 2
    for slot in range(CORES):
        weights = row_weights(mix_ref, where_ref, backs, depth, slot)
        hidden_cot = weights * dot_columns(c_buf[...], downs[slot][...])
        gate = pre_ref[:, slot * width : slot * width + units]
        up = pre_ref[:, slot * width + units : (slot + 1) * width]
        sigma = jax.nn.sigmoid(gate)
        silu = gate * sigma
        h_buf[slot] = (weights * (silu * up)).astype(BF16)
        slope = sigma * (1.0 + gate * (1.0 - sigma))
        g_buf[slot, :, :units] = (hidden_cot * up * slope).astype(BF16)
        g_buf[slot, :, units:] = (hidden_cot * silu).astype(BF16)
        for number, (buf, to) in enumerate(((h_buf, hid_all), (g_buf, pre_all))):
            copies.append(pltpu.make_async_copy(buf.at[slot], to.at[slot, at], sems.at[slot, number]))
            copies[-1].start()
    for copy in copies:
        copy.wait()


def backward(backs, depth, where, pairs, fars, pre, mix, downs, kept):
    rows, half = pairs[0].shape[1:]
    width = pre.shape[1] // 2
    total = 2 * rows * len(backs)
    every = 2 * rows * depth
    fresh = kept is None
    first = 2 * len(backs) + 5
    vmem = pl.BlockSpec(memory_space=pltpu.VMEM)
    hbm = pl.BlockSpec(memory_space=pl.ANY)
    return pl.pallas_call(
        functools.partial(backward_kernel, backs, depth, fresh),
        out_shape=(
            jax.ShapeDtypeStruct((every, 2 * half), BF16),
            jax.ShapeDtypeStruct((CORES, every, width // 2), BF16),
            jax.ShapeDtypeStruct((CORES, every, width), BF16),
        ),
        in_specs=[pl.BlockSpec(memory_space=pltpu.SMEM)]
        + [vmem] * (first - 1)
        + ([] if fresh else [hbm] * 3),
        out_specs=(hbm,) * 3,
        input_output_aliases={} if fresh else {first: 0, first + 1: 1, first + 2: 2},
        scratch_shapes=[
            pltpu.VMEM((total, 2 * half), BF16),
            pltpu.VMEM((CORES, total, width // 2), BF16),
            pltpu.VMEM((CORES, total, width), BF16),
            pltpu.SemaphoreType.DMA((CORES + 1, 2)),
        ],
        compiler_params=pltpu.CompilerParams(vmem_limit_bytes=16 << 20),
        cost_estimate=pl.CostEstimate(
            flops=2 * total * half * width * 2, bytes_accessed=20 * total * half, transcendentals=total * width
        ),
    )(where, *pairs, *fars, pre, mix, *downs, *([] if fresh else kept))


def in_grads_kernel(rows_ref, pre_ref, *refs):
    grads = dot_rows(rows_ref[...], pre_ref[0])
    if len(refs) == 1:
        refs[0][...] = grads.astype(BF16)
        return
    got, gate_ref, up_ref = refs
    grads += got[...].astype(F32)
    units = gate_ref.shape[1]
    gate_ref[...] = grads[:, :units].astype(BF16)
    up_ref[...] = grads[:, units:].astype(BF16)


def down_grads_kernel(cot_ref, hid_ref, *refs):
    grads = dot_rows(hid_ref[0], cot_ref[...])
    if len(refs) == 2:
        grads += refs[0][...].astype(F32)
    refs[-1][...] = grads.astype(BF16)


def in_grads(slot, rows_all, pre_all, got=None):
    total, features = rows_all.shape
    width = pre_all.shape[2]
    tile = min(TILE, features)

    def tall(columns):
        return pl.BlockSpec((tile, columns), lambda i: (i, 0))

    columns = (width,) if got is None else (width // 2, width // 2)
    return pl.pallas_call(
        in_grads_kernel,
        grid=(features // tile,),
        out_shape=tuple(jax.ShapeDtypeStruct((features, some), BF16) for some in columns),
        in_specs=[
            pl.BlockSpec((total, tile), lambda i: (0, i)),
            pl.BlockSpec((1, total, width), lambda i: (slot, 0, 0)),
        ]
        + ([] if got is None else [tall(width)]),
        out_specs=tuple(tall(some) for some in columns),
        compiler_params=pltpu.CompilerParams(vmem_limit_bytes=20 << 20),
        cost_estimate=pl.CostEstimate(
            flops=2 * total * features * width, bytes_accessed=2 * features * (total + width), transcendentals=0
        ),
    )(rows_all, pre_all, *([] if got is None else [got]))


def down_grads(slot, cot_all, hid_all, got=None):
    total, features = cot_all.shape
    units = hid_all.shape[2]
    tile = min(TILE, features)
    flat = pl.BlockSpec((units, tile), lambda i: (0, i))
    return pl.pallas_call(
        down_grads_kernel,
        grid=(features // tile,),
        out_shape=jax.ShapeDtypeStruct((units, features), BF16),
        in_specs=[
            pl.BlockSpec((total, tile), lambda i: (0, i)),
            pl.BlockSpec((1, total, units), lambda i: (slot, 0, 0)),
        ]
        + ([] if got is None else [flat]),
        out_specs=flat,
        compiler_params=pltpu.CompilerParams(vmem_limit_bytes=16 << 20),
        cost_estimate=pl.CostEstimate(
            flops=2 * total * features * units, bytes_accessed=2 * features * (total + units), transcendentals=0
        ),
    )(cot_all, hid_all, *([] if got is None else [got]))


def gather_plan(tokens, cotangent, routes, gate_probs, matching, gate_weight, up_weight, down_weight):
    expert_count = lax.axis_size("expert")
    depth, shift, swap, first, second = moves(expert_count)

    def send(value, pairs):
        return lax.ppermute(value, AXES, pairs)

    y, at = lax.axis_index("dp"), lax.axis_index("expert")
    where = jnp.stack([y, at // (SIDE * CORES), (at // CORES) % SIDE, at % CORES]).astype(jnp.int32)

    down = down_weight[0]
    downs = (down, send(down, swap))
    in_weight = jnp.concatenate([gate_weight[0], up_weight[0]], axis=1)
    ins = (in_weight, send(in_weight, swap))

    groups = [tuple(range(at, min(at + GROUP, depth))) for at in range(0, depth, GROUP)]

    along = [tokens]
    for _ in range(1, depth):
        along.append(send(along[-1], shift[1]))
    around = []
    for piece in along:
        piece = piece[None]
        a = send(piece, first)
        b = send(piece, second)
        d = send(a, second)
        around.append((piece, a, b, d))
    sets = [[around[back] for back in backs] for backs in groups]

    pairs = [jnp.stack([cotangent, send(cotangent, first)])]
    for _ in range(1, depth):
        pairs.append(send(pairs[-1], shift[1]))
    fars = [send(pair, second) for pair in pairs]

    mix = gate_probs / jnp.sum(gate_probs, axis=1, keepdims=True)
    hit = routes[:, :, None] == jnp.arange(matching.shape[0], dtype=jnp.int32)
    host = jnp.sum(jnp.where(hit, matching, 0), axis=2)
    slots = jnp.arange(expert_count, dtype=jnp.int32)
    slots = (slots[:, None] // CORES * CORES + jnp.arange(CORES, dtype=jnp.int32)).reshape(-1)
    per_slot = jnp.sum(jnp.where(host[None] == slots[:, None, None], mix[None], 0.0), axis=2)
    mix = lax.all_to_all(per_slot, "expert", split_axis=0, concat_axis=0, tiled=True)
    mix = mix.T

    rows_all, pres, out = None, [], None
    for number, backs in enumerate(groups):
        *got, pre, rows_all = forward(
            backs, depth, where, sets[number], mix, ins, downs, rows_all
        )
        pres.append(pre)
        own, a, b, d = got
        d = send(d, second)
        b = send(b, second)
        a = (a.astype(F32) + d).astype(BF16)
        a = send(a, first)
        own = own.astype(F32) + a + b
        for member, back in enumerate(backs):
            part = own[member]
            if back:
                part = send(part.astype(BF16), shift[-back]).astype(F32)
            out = part if out is None else out + part

    kept = None
    for number, backs in enumerate(groups):
        some = slice(backs[0], backs[-1] + 1)
        kept = backward(
            backs, depth, where, pairs[some], fars[some], pres[number], mix, downs, kept
        )
    cot_all, hid_all, pre_all = kept
    (in_got,) = in_grads(1, rows_all, pre_all)
    in_got = send(in_got, swap)
    down_got = down_grads(1, cot_all, hid_all)
    down_got = send(down_got, swap)
    gate_grad, up_grad = in_grads(0, rows_all, pre_all, in_got)
    down_grad = down_grads(0, cot_all, hid_all, down_got)
    out = out.astype(BF16)
    return out, gate_grad[None], up_grad[None], down_grad[None]


def solution(mesh):
    experts = mesh.shape["expert"]
    square = mesh.shape["dp"] == 2 and experts % (SIDE * CORES) == 0

    def on_device(*args):
        dense = 2 * args[2].shape[1] >= experts
        if not (square and dense):
            return exchange_plan(*args)
        return gather_plan(*args)

    placed = (
        P("expert", "dp"),
        P("expert", "dp"),
        P("expert", None),
        P("expert", None),
        P(),
        P("expert", None, "dp"),
        P("expert", None, "dp"),
        P("expert", "dp", None),
    )
    return jax.shard_map(
        on_device,
        mesh=mesh,
        in_specs=placed,
        out_specs=(
            P("expert", "dp"),
            P("expert", None, "dp"),
            P("expert", None, "dp"),
            P("expert", "dp", None),
        ),
        check_vma=False,
    )
```

```python
import functools

import jax
import jax.numpy as jnp
from jax import lax
from jax.experimental import pallas as pl
from jax.experimental.pallas import tpu as pltpu
from jax.sharding import PartitionSpec as P


AXES = ("dp", "expert")
CORES = 2
SIDE = 2
GROUP = 2
ALONG = {3: -1}
TILE = 512
F32 = jnp.float32
BF16 = jnp.bfloat16


def exchange_plan(tokens, cotangent, routes, gate_probs, matching, gate_weight, up_weight, down_weight):
    expert_count = lax.axis_size("expert")
    token_count, fan_out = routes.shape
    capacity = max(2, token_count * fan_out * 9 // (8 * expert_count))
    route_count = token_count * fan_out
    mix_weights = gate_probs / jnp.sum(gate_probs, axis=1, keepdims=True)
    flat_routes = routes.reshape(-1)
    expert_hit = flat_routes[:, None] == jnp.arange(matching.shape[0], dtype=jnp.int32)[None, :]
    host_of = jnp.sum(jnp.where(expert_hit, matching[None, :], 0), axis=1)
    host_hit = (host_of[:, None] == jnp.arange(expert_count, dtype=jnp.int32)[None, :]).astype(
        jnp.int32
    )
    running = jnp.cumsum(host_hit, axis=0)
    slot_rank = jnp.sum((running - 1) * host_hit, axis=1)
    position = host_of * capacity + slot_rank
    slot_table = (
        jnp.full((expert_count * capacity,), route_count, jnp.int32)
        .at[position]
        .set(jnp.arange(route_count, dtype=jnp.int32))
    )
    filled = slot_table < route_count
    route_ids = jnp.minimum(slot_table, route_count - 1)
    token_ids = jnp.where(filled, route_ids // fan_out, token_count)
    clamped_ids = route_ids // fan_out
    slot_mix = jnp.where(filled, jnp.take(mix_weights.reshape(-1), route_ids), 0.0)
    recv_rows = lax.all_to_all(
        jnp.take(tokens, token_ids, axis=0, mode="fill", fill_value=0),
        "expert",
        split_axis=0,
        concat_axis=0,
        tiled=True,
    )
    gathered = jnp.take(cotangent, clamped_ids, axis=0)
    recv_cot = lax.all_to_all(
        (slot_mix[:, None] * gathered.astype(jnp.float32)).astype(jnp.bfloat16),
        "expert",
        split_axis=0,
        concat_axis=0,
        tiled=True,
    )
    inputs, out_cot = (
        lax.all_gather(recv_rows, "dp", axis=1, tiled=True),
        lax.all_gather(recv_cot, "dp", axis=1, tiled=True),
    )
    gate_pre = jnp.dot(inputs, gate_weight[0], preferred_element_type=jnp.float32)
    up_pre = jnp.dot(inputs, up_weight[0], preferred_element_type=jnp.float32)
    sigma_gate = jax.nn.sigmoid(gate_pre)
    silu_gate = gate_pre * sigma_gate
    hidden = (silu_gate * up_pre).astype(jnp.bfloat16)
    partial_out = jnp.dot(hidden, down_weight[0], preferred_element_type=jnp.float32)
    contract_rows = (((0,), (0,)), ((), ()))
    down_grad = lax.dot_general(
        hidden, out_cot, contract_rows, preferred_element_type=jnp.float32
    ).astype(jnp.bfloat16)
    hidden_cot = lax.dot_general(
        out_cot, down_weight[0], (((1,), (1,)), ((), ())), preferred_element_type=jnp.float32
    )
    slope = sigma_gate * (1.0 + gate_pre * (1.0 - sigma_gate))
    gate_cot = (hidden_cot * up_pre * slope).astype(jnp.bfloat16)
    up_cot = (hidden_cot * silu_gate).astype(jnp.bfloat16)
    gate_grad = lax.dot_general(
        inputs, gate_cot, contract_rows, preferred_element_type=jnp.float32
    ).astype(jnp.bfloat16)
    up_grad = lax.dot_general(
        inputs, up_cot, contract_rows, preferred_element_type=jnp.float32
    ).astype(jnp.bfloat16)
    summed = lax.psum_scatter(
        partial_out.astype(jnp.bfloat16), "dp", scatter_dimension=1, tiled=True
    )
    merged = lax.all_to_all(summed, "expert", split_axis=0, concat_axis=0, tiled=True)
    half_width = merged.shape[1]
    expert_out = jnp.take(merged, position, axis=0).reshape(token_count, fan_out, half_width)
    layer_out = jnp.sum(mix_weights[:, :, None] * expert_out.astype(jnp.float32), axis=1).astype(
        jnp.bfloat16
    )
    return (layer_out, gate_grad[None], up_grad[None], down_grad[None])


def moves(expert_count):
    depth = expert_count // (SIDE * CORES)

    def table(step):
        pairs = []
        for y in range(2):
            for z in range(depth):
                for x in range(SIDE):
                    for core in range(CORES):
                        ty, tz, tx, tcore = step(y, z, x, core)
                        pairs.append(
                            (
                                y * expert_count + (z * SIDE + x) * CORES + core,
                                ty * expert_count + (tz * SIDE + tx) * CORES + tcore,
                            )
                        )
        return pairs

    shift = {
        by: table(lambda y, z, x, core, by=by: (y, (z + by) % depth, x, core))
        for by in range(1 - depth, depth)
        if by
    }
    swap = table(lambda y, z, x, core: (y, z, x, 1 - core))
    first = table(lambda y, z, x, core: (y, z, 1 - x, core) if core == 0 else (1 - y, z, x, core))
    second = table(lambda y, z, x, core: (1 - y, z, x, core) if core == 0 else (y, z, 1 - x, core))
    return depth, shift, swap, first, second


def dot(a, b):
    return jnp.dot(a, b, preferred_element_type=F32)


def dot_rows(a, b):
    return lax.dot_general(a, b, (((0,), (0,)), ((), ())), preferred_element_type=F32)


def dot_columns(a, b):
    return lax.dot_general(a, b, (((1,), (1,)), ((), ())), preferred_element_type=F32)


def piece_windows(where_ref, member, rows, half):
    y, core = where_ref[0], where_ref[3]

    def window(lower, other):
        side = jnp.where(other == 1, 1 - y, y)
        return (
            pl.ds(pl.multiple_of((2 * member + lower) * rows, rows), rows),
            pl.ds(pl.multiple_of(side * half, half), half),
        )

    return window(0, 0), window(1 - core, core), window(core, 1 - core), window(1, 1)


def row_weights(mix_ref, where_ref, backs, depth, slot):
    core, x = where_ref[3], where_ref[2]
    parity = core if slot == 0 else 1 - core
    rows = mix_ref.shape[1]
    down = lax.broadcasted_iota(jnp.int32, (rows, rows), 0)
    along = lax.broadcasted_iota(jnp.int32, (rows, rows), 1)
    columns = []
    for back in backs:
        z = lax.rem(where_ref[1] + depth - back, depth)
        for across in (x, 1 - x):
            block = (z * SIDE + across) * CORES + core
            row = mix_ref[pl.ds(block * CORES + parity, 1), :]
            columns.append(jnp.sum(jnp.where(down == along, row, 0.0), axis=1, keepdims=True))
    return jnp.concatenate(columns, axis=0)


def forward_kernel(backs, depth, sets, where_ref, *refs):
    pieces, refs = refs[: 4 * sets], refs[4 * sets :]
    mix_ref, ins, downs, refs = refs[0], refs[1:3], refs[3:5], refs[5:]
    outs, pre_ref, rows_ref, x_buf, o_buf, sem = refs[:4], refs[4], refs[5], refs[6], refs[7], refs[8]
    rows, half = pieces[0].shape[1:]
    member = 0
    for number in range(sets):
        group = pieces[4 * number : 4 * number + 4]
        for inner in range(group[0].shape[0]):
            for window, piece in zip(piece_windows(where_ref, member, rows, half), group):
                x_buf[window] = piece[inner]
            member += 1
    keep = pltpu.make_async_copy(x_buf, rows_ref, sem)
    keep.start()
    width = ins[0].shape[1]
    units = width // 2
    cut = width * 2 // 3
    for slot in range(CORES):
        pre_ref[:, slot * width : slot * width + cut] = dot(x_buf[...], ins[slot][:, :cut])
    last = dot(x_buf[...], jnp.concatenate([ins[0][:, cut:], ins[1][:, cut:]], axis=1))
    pre_ref[:, cut:width] = last[:, : width - cut]
    pre_ref[:, width + cut :] = last[:, width - cut :]
    hiddens = []
    for slot in range(CORES):
        gate = pre_ref[:, slot * width : slot * width + units]
        up = pre_ref[:, slot * width + units : (slot + 1) * width]
        weights = row_weights(mix_ref, where_ref, backs, depth, slot)
        hiddens.append((weights * (gate * jax.nn.sigmoid(gate) * up)).astype(BF16))
    o_buf[...] = dot(
        jnp.concatenate(hiddens, axis=1), jnp.concatenate([downs[0][...], downs[1][...]], axis=0)
    ).astype(BF16)
    for member in range(len(backs)):
        for window, ref in zip(piece_windows(where_ref, member, rows, half), outs):
            ref[member] = o_buf[window]
    keep.wait()


def forward(backs, depth, where, sets, mix, ins, downs):
    rows, half = sets[0][0].shape[1:]
    width = ins[0].shape[1]
    total = 2 * rows * len(backs)
    flat = [piece for pieces in sets for piece in pieces]
    vmem = pl.BlockSpec(memory_space=pltpu.VMEM)
    hbm = pl.BlockSpec(memory_space=pl.ANY)
    return pl.pallas_call(
        functools.partial(forward_kernel, backs, depth, len(sets)),
        out_shape=tuple([jax.ShapeDtypeStruct((len(backs), rows, half), BF16)] * 4)
        + (
            jax.ShapeDtypeStruct((total, CORES * width), F32),
            jax.ShapeDtypeStruct((total, 2 * half), BF16),
        ),
        in_specs=[pl.BlockSpec(memory_space=pltpu.SMEM)] + [vmem] * (len(flat) + 5),
        out_specs=(vmem,) * 5 + (hbm,),
        scratch_shapes=[
            pltpu.VMEM((total, 2 * half), BF16),
            pltpu.VMEM((total, 2 * half), BF16),
            pltpu.SemaphoreType.DMA,
        ],
        compiler_params=pltpu.CompilerParams(vmem_limit_bytes=14 << 20),
        cost_estimate=pl.CostEstimate(
            flops=2 * total * half * width * 6, bytes_accessed=12 * total * half, transcendentals=total * width
        ),
    )(where, *flat, mix, *ins, *downs)


def backward_kernel(backs, depth, where_ref, *refs):
    count = len(backs)
    pairs, fars, refs = refs[:count], refs[count : 2 * count], refs[2 * count :]
    pre_ref, mix_ref, downs, refs = refs[0], refs[1], refs[2:4], refs[4:]
    cot_ref, hid_ref, both_ref, c_buf, h_buf, g_buf, sems = refs
    rows, half = pairs[0].shape[1:]
    for member in range(count):
        pieces = (pairs[member].at[0], pairs[member].at[1], fars[member].at[0], fars[member].at[1])
        for window, piece in zip(piece_windows(where_ref, member, rows, half), pieces):
            c_buf[window] = piece[...]
    copies = [pltpu.make_async_copy(c_buf, cot_ref, sems.at[CORES, 0])]
    copies[0].start()
    width = pre_ref.shape[1] // 2
    units = width // 2
    for slot in range(CORES):
        weights = row_weights(mix_ref, where_ref, backs, depth, slot)
        hidden_cot = weights * dot_columns(c_buf[...], downs[slot][...])
        gate = pre_ref[:, slot * width : slot * width + units]
        up = pre_ref[:, slot * width + units : (slot + 1) * width]
        sigma = jax.nn.sigmoid(gate)
        silu = gate * sigma
        h_buf[slot] = (weights * (silu * up)).astype(BF16)
        slope = sigma * (1.0 + gate * (1.0 - sigma))
        g_buf[slot, :, :units] = (hidden_cot * up * slope).astype(BF16)
        g_buf[slot, :, units:] = (hidden_cot * silu).astype(BF16)
        for number, (buf, to) in enumerate(((h_buf, hid_ref), (g_buf, both_ref))):
            copies.append(pltpu.make_async_copy(buf.at[slot], to.at[slot], sems.at[slot, number]))
            copies[-1].start()
    for copy in copies:
        copy.wait()


def backward(backs, depth, where, pairs, fars, pre, mix, downs):
    rows, half = pairs[0].shape[1:]
    width = pre.shape[1] // 2
    total = 2 * rows * len(backs)
    vmem = pl.BlockSpec(memory_space=pltpu.VMEM)
    hbm = pl.BlockSpec(memory_space=pl.ANY)
    return pl.pallas_call(
        functools.partial(backward_kernel, backs, depth),
        out_shape=(
            jax.ShapeDtypeStruct((total, 2 * half), BF16),
            jax.ShapeDtypeStruct((CORES, total, width // 2), BF16),
            jax.ShapeDtypeStruct((CORES, total, width), BF16),
        ),
        in_specs=[pl.BlockSpec(memory_space=pltpu.SMEM)] + [vmem] * (2 * len(backs) + 4),
        out_specs=(hbm,) * 3,
        scratch_shapes=[
            pltpu.VMEM((total, 2 * half), BF16),
            pltpu.VMEM((CORES, total, width // 2), BF16),
            pltpu.VMEM((CORES, total, width), BF16),
            pltpu.SemaphoreType.DMA((CORES + 1, 2)),
        ],
        compiler_params=pltpu.CompilerParams(vmem_limit_bytes=12 << 20),
        cost_estimate=pl.CostEstimate(
            flops=2 * total * half * width * 2, bytes_accessed=20 * total * half, transcendentals=total * width
        ),
    )(where, *pairs, *fars, pre, mix, *downs)


def grads_kernel(added, left_ref, right_ref, *refs):
    left = left_ref[...] if left_ref.ndim == 2 else left_ref[0]
    right = right_ref[...] if right_ref.ndim == 2 else right_ref[0]
    grads = dot_rows(left, right)
    for ref in refs[:added]:
        grads += ref[...].astype(F32)
    outs = refs[added:]
    columns = outs[0].shape[1]
    for number, ref in enumerate(outs):
        ref[...] = grads[:, number * columns : (number + 1) * columns].astype(ref.dtype)


def in_grads(slot, rows_ref, both, add, kinds):
    total, features = rows_ref.shape
    width = both.shape[2]
    tile = min(TILE, features)

    def tall(columns):
        return pl.BlockSpec((tile, columns), lambda i: (i, 0))

    columns = width // len(kinds)
    return pl.pallas_call(
        functools.partial(grads_kernel, len(add)),
        grid=(features // tile,),
        out_shape=tuple(jax.ShapeDtypeStruct((features, columns), kind) for kind in kinds),
        in_specs=[
            pl.BlockSpec((total, tile), lambda i: (0, i)),
            pl.BlockSpec((1, total, width), lambda i: (slot, 0, 0)),
        ]
        + [tall(width)] * len(add),
        out_specs=tuple(tall(columns) for _ in kinds),
        compiler_params=pltpu.CompilerParams(vmem_limit_bytes=20 << 20),
        cost_estimate=pl.CostEstimate(
            flops=2 * total * features * width, bytes_accessed=2 * features * (total + width), transcendentals=0
        ),
    )(rows_ref, both, *add)


def down_grads(slot, cot, hid, add, kind):
    total, features = cot.shape
    units = hid.shape[2]
    tile = min(TILE, features)
    flat = pl.BlockSpec((units, tile), lambda i: (0, i))
    return pl.pallas_call(
        functools.partial(grads_kernel, len(add)),
        grid=(features // tile,),
        out_shape=(jax.ShapeDtypeStruct((units, features), kind),),
        in_specs=[
            pl.BlockSpec((1, total, units), lambda i: (slot, 0, 0)),
            pl.BlockSpec((total, tile), lambda i: (0, i)),
        ]
        + [flat] * len(add),
        out_specs=(flat,),
        compiler_params=pltpu.CompilerParams(vmem_limit_bytes=16 << 20),
        cost_estimate=pl.CostEstimate(
            flops=2 * total * features * units, bytes_accessed=2 * features * (total + units), transcendentals=0
        ),
    )(hid, cot, *add)


def gather_plan(tokens, cotangent, routes, gate_probs, matching, gate_weight, up_weight, down_weight):
    expert_count = lax.axis_size("expert")
    depth, shift, swap, first, second = moves(expert_count)

    def send(value, pairs):
        return lax.ppermute(value, AXES, pairs)

    rows, _ = tokens.shape
    y, at = lax.axis_index("dp"), lax.axis_index("expert")
    where = jnp.stack([y, at // (SIDE * CORES), (at // CORES) % SIDE, at % CORES]).astype(jnp.int32)

    down = down_weight[0]
    downs = (down, send(down, swap))
    in_weight = jnp.concatenate([gate_weight[0], up_weight[0]], axis=1)
    ins = (in_weight, send(in_weight, swap))

    groups = [tuple(range(at, min(at + GROUP, depth))) for at in range(0, depth, GROUP)]

    along = [tokens]
    for _ in range(1, depth):
        along.append(send(along[-1], shift[1]))
    around = []
    for piece in along:
        piece = piece[None]
        a = send(piece, first)
        b = send(piece, second)
        d = send(a, second)
        around.append((piece, a, b, d))
    sets = [[around[back] for back in backs] for backs in groups]

    pairs = [jnp.stack([cotangent, send(cotangent, first)])]
    late = depth // 2
    for back in range(1, depth):
        if back > late:
            pairs.append(send(pairs[0], shift[back - depth]))
        else:
            pairs.append(send(pairs[-1], shift[1]))
    fars = []
    for back, pair in enumerate(pairs):
        if back in ALONG:
            fars.append(send(fars[0], shift[ALONG[back]]))
        else:
            fars.append(send(pair, second))

    mix = gate_probs / jnp.sum(gate_probs, axis=1, keepdims=True)
    hit = routes[:, :, None] == jnp.arange(matching.shape[0], dtype=jnp.int32)
    host = jnp.sum(jnp.where(hit, matching, 0), axis=2)
    slots = jnp.arange(expert_count, dtype=jnp.int32)
    slots = (slots[:, None] // CORES * CORES + jnp.arange(CORES, dtype=jnp.int32)).reshape(-1)
    per_slot = jnp.sum(jnp.where(host[None] == slots[:, None, None], mix[None], 0.0), axis=2)
    mix = lax.all_to_all(per_slot, "expert", split_axis=0, concat_axis=0, tiled=True)
    mix = mix.reshape(CORES * expert_count, rows)

    kept_rows, pres, out = [], [], None
    for number, backs in enumerate(groups):
        *got, pre, kept = forward(backs, depth, where, sets[number], mix, ins, downs)
        pres.append(pre)
        kept_rows.append(kept)
        own, a, b, d = got
        d = send(d, second)
        b = send(b, second)
        a = (a.astype(F32) + d).astype(BF16)
        a = send(a, first)
        own = own.astype(F32) + a + b
        for member, back in enumerate(backs):
            part = own[member]
            if back:
                part = send(part.astype(BF16), shift[-back]).astype(F32)
            out = part if out is None else out + part

    in_sums, down_sums = [[], []], [[], []]
    for number, backs in enumerate(groups):
        some = slice(backs[0], backs[-1] + 1)
        cot, hid, both = backward(
            backs, depth, where, pairs[some], fars[some], pres[number], mix, downs
        )
        if number == len(groups) - 1:
            break
        for slot in (1, 0):
            in_sums[slot] = in_grads(slot, kept_rows[number], both, in_sums[slot], (F32,))
            down_sums[slot] = down_grads(slot, cot, hid, down_sums[slot], F32)
    (in_got,) = in_grads(1, kept_rows[-1], both, in_sums[1], (BF16,))
    in_got = send(in_got, swap)
    (down_got,) = down_grads(1, cot, hid, down_sums[1], BF16)
    down_got = send(down_got, swap)
    gate_grad, up_grad = in_grads(0, kept_rows[-1], both, [*in_sums[0], in_got], (BF16, BF16))
    (down_grad,) = down_grads(0, cot, hid, [*down_sums[0], down_got], BF16)
    out = out.astype(BF16)
    return out, gate_grad[None], up_grad[None], down_grad[None]


def solution(mesh):
    experts = mesh.shape["expert"]
    square = mesh.shape["dp"] == 2 and experts % (SIDE * CORES) == 0

    def on_device(*args):
        dense = 2 * args[2].shape[1] >= experts
        if not (square and dense):
            return exchange_plan(*args)
        return gather_plan(*args)

    placed = (
        P("expert", "dp"),
        P("expert", "dp"),
        P("expert", None),
        P("expert", None),
        P(),
        P("expert", None, "dp"),
        P("expert", None, "dp"),
        P("expert", "dp", None),
    )
    return jax.shard_map(
        on_device,
        mesh=mesh,
        in_specs=placed,
        out_specs=(
            P("expert", "dp"),
            P("expert", None, "dp"),
            P("expert", None, "dp"),
            P("expert", "dp", None),
        ),
        check_vma=False,
    )
```

```python
import functools

import jax
import jax.numpy as jnp
from jax import lax
from jax.experimental import pallas as pl
from jax.experimental.pallas import tpu as pltpu
from jax.sharding import PartitionSpec as P


AXES = ("dp", "expert")
CORES = 2
SIDE = 2
GROUP = 2
ALONG = {3: (0, -1), 2: (1, 1)}
TILE = 512
F32 = jnp.float32
BF16 = jnp.bfloat16


def exchange_plan(tokens, cotangent, routes, gate_probs, matching, gate_weight, up_weight, down_weight):
    expert_count = lax.axis_size("expert")
    token_count, fan_out = routes.shape
    capacity = max(2, token_count * fan_out * 9 // (8 * expert_count))
    route_count = token_count * fan_out
    mix_weights = gate_probs / jnp.sum(gate_probs, axis=1, keepdims=True)
    flat_routes = routes.reshape(-1)
    expert_hit = flat_routes[:, None] == jnp.arange(matching.shape[0], dtype=jnp.int32)[None, :]
    host_of = jnp.sum(jnp.where(expert_hit, matching[None, :], 0), axis=1)
    host_hit = (host_of[:, None] == jnp.arange(expert_count, dtype=jnp.int32)[None, :]).astype(
        jnp.int32
    )
    running = jnp.cumsum(host_hit, axis=0)
    slot_rank = jnp.sum((running - 1) * host_hit, axis=1)
    position = host_of * capacity + slot_rank
    slot_table = (
        jnp.full((expert_count * capacity,), route_count, jnp.int32)
        .at[position]
        .set(jnp.arange(route_count, dtype=jnp.int32))
    )
    filled = slot_table < route_count
    route_ids = jnp.minimum(slot_table, route_count - 1)
    token_ids = jnp.where(filled, route_ids // fan_out, token_count)
    clamped_ids = route_ids // fan_out
    slot_mix = jnp.where(filled, jnp.take(mix_weights.reshape(-1), route_ids), 0.0)
    recv_rows = lax.all_to_all(
        jnp.take(tokens, token_ids, axis=0, mode="fill", fill_value=0),
        "expert",
        split_axis=0,
        concat_axis=0,
        tiled=True,
    )
    gathered = jnp.take(cotangent, clamped_ids, axis=0)
    recv_cot = lax.all_to_all(
        (slot_mix[:, None] * gathered.astype(jnp.float32)).astype(jnp.bfloat16),
        "expert",
        split_axis=0,
        concat_axis=0,
        tiled=True,
    )
    inputs, out_cot = (
        lax.all_gather(recv_rows, "dp", axis=1, tiled=True),
        lax.all_gather(recv_cot, "dp", axis=1, tiled=True),
    )
    gate_pre = jnp.dot(inputs, gate_weight[0], preferred_element_type=jnp.float32)
    up_pre = jnp.dot(inputs, up_weight[0], preferred_element_type=jnp.float32)
    sigma_gate = jax.nn.sigmoid(gate_pre)
    silu_gate = gate_pre * sigma_gate
    hidden = (silu_gate * up_pre).astype(jnp.bfloat16)
    partial_out = jnp.dot(hidden, down_weight[0], preferred_element_type=jnp.float32)
    contract_rows = (((0,), (0,)), ((), ()))
    down_grad = lax.dot_general(
        hidden, out_cot, contract_rows, preferred_element_type=jnp.float32
    ).astype(jnp.bfloat16)
    hidden_cot = lax.dot_general(
        out_cot, down_weight[0], (((1,), (1,)), ((), ())), preferred_element_type=jnp.float32
    )
    slope = sigma_gate * (1.0 + gate_pre * (1.0 - sigma_gate))
    gate_cot = (hidden_cot * up_pre * slope).astype(jnp.bfloat16)
    up_cot = (hidden_cot * silu_gate).astype(jnp.bfloat16)
    gate_grad = lax.dot_general(
        inputs, gate_cot, contract_rows, preferred_element_type=jnp.float32
    ).astype(jnp.bfloat16)
    up_grad = lax.dot_general(
        inputs, up_cot, contract_rows, preferred_element_type=jnp.float32
    ).astype(jnp.bfloat16)
    summed = lax.psum_scatter(
        partial_out.astype(jnp.bfloat16), "dp", scatter_dimension=1, tiled=True
    )
    merged = lax.all_to_all(summed, "expert", split_axis=0, concat_axis=0, tiled=True)
    half_width = merged.shape[1]
    expert_out = jnp.take(merged, position, axis=0).reshape(token_count, fan_out, half_width)
    layer_out = jnp.sum(mix_weights[:, :, None] * expert_out.astype(jnp.float32), axis=1).astype(
        jnp.bfloat16
    )
    return (layer_out, gate_grad[None], up_grad[None], down_grad[None])


def moves(expert_count):
    depth = expert_count // (SIDE * CORES)

    def table(step):
        pairs = []
        for y in range(2):
            for z in range(depth):
                for x in range(SIDE):
                    for core in range(CORES):
                        ty, tz, tx, tcore = step(y, z, x, core)
                        pairs.append(
                            (
                                y * expert_count + (z * SIDE + x) * CORES + core,
                                ty * expert_count + (tz * SIDE + tx) * CORES + tcore,
                            )
                        )
        return pairs

    shift = {
        by: table(lambda y, z, x, core, by=by: (y, (z + by) % depth, x, core))
        for by in range(1 - depth, depth)
        if by
    }
    swap = table(lambda y, z, x, core: (y, z, x, 1 - core))
    first = table(lambda y, z, x, core: (y, z, 1 - x, core) if core == 0 else (1 - y, z, x, core))
    second = table(lambda y, z, x, core: (1 - y, z, x, core) if core == 0 else (y, z, 1 - x, core))
    return depth, shift, swap, first, second


def dot(a, b):
    return jnp.dot(a, b, preferred_element_type=F32)


def dot_rows(a, b):
    return lax.dot_general(a, b, (((0,), (0,)), ((), ())), preferred_element_type=F32)


def dot_columns(a, b):
    return lax.dot_general(a, b, (((1,), (1,)), ((), ())), preferred_element_type=F32)


def piece_windows(where_ref, member, rows, half):
    y, core = where_ref[0], where_ref[3]

    def window(lower, other):
        side = jnp.where(other == 1, 1 - y, y)
        return (
            pl.ds(pl.multiple_of((2 * member + lower) * rows, rows), rows),
            pl.ds(pl.multiple_of(side * half, half), half),
        )

    return window(0, 0), window(1 - core, core), window(core, 1 - core), window(1, 1)


def row_weights(mix_ref, where_ref, backs, depth, slot):
    core, x = where_ref[3], where_ref[2]
    parity = core if slot == 0 else 1 - core
    rows = mix_ref.shape[1]
    down = lax.broadcasted_iota(jnp.int32, (rows, rows), 0)
    along = lax.broadcasted_iota(jnp.int32, (rows, rows), 1)
    columns = []
    for back in backs:
        z = lax.rem(where_ref[1] + depth - back, depth)
        for across in (x, 1 - x):
            block = (z * SIDE + across) * CORES + core
            row = mix_ref[pl.ds(block * CORES + parity, 1), :]
            columns.append(jnp.sum(jnp.where(down == along, row, 0.0), axis=1, keepdims=True))
    return jnp.concatenate(columns, axis=0)


def forward_kernel(backs, depth, sets, where_ref, *refs):
    pieces, refs = refs[: 4 * sets], refs[4 * sets :]
    mix_ref, ins, downs, refs = refs[0], refs[1:3], refs[3:5], refs[5:]
    outs, pre_ref, rows_ref, x_buf, o_buf, sem = refs[:4], refs[4], refs[5], refs[6], refs[7], refs[8]
    rows, half = pieces[0].shape[1:]
    member = 0
    for number in range(sets):
        group = pieces[4 * number : 4 * number + 4]
        for inner in range(group[0].shape[0]):
            for window, piece in zip(piece_windows(where_ref, member, rows, half), group):
                x_buf[window] = piece[inner]
            member += 1
    keep = pltpu.make_async_copy(x_buf, rows_ref, sem)
    keep.start()
    width = ins[0].shape[1]
    units = width // 2
    cut = width * 2 // 3
    for slot in range(CORES):
        pre_ref[:, slot * width : slot * width + cut] = dot(x_buf[...], ins[slot][:, :cut])
    last = dot(x_buf[...], jnp.concatenate([ins[0][:, cut:], ins[1][:, cut:]], axis=1))
    pre_ref[:, cut:width] = last[:, : width - cut]
    pre_ref[:, width + cut :] = last[:, width - cut :]
    hiddens = []
    for slot in range(CORES):
        gate = pre_ref[:, slot * width : slot * width + units]
        up = pre_ref[:, slot * width + units : (slot + 1) * width]
        weights = row_weights(mix_ref, where_ref, backs, depth, slot)
        hiddens.append((weights * (gate * jax.nn.sigmoid(gate) * up)).astype(BF16))
    o_buf[...] = dot(
        jnp.concatenate(hiddens, axis=1), jnp.concatenate([downs[0][...], downs[1][...]], axis=0)
    ).astype(BF16)
    for member in range(len(backs)):
        for window, ref in zip(piece_windows(where_ref, member, rows, half), outs):
            ref[member] = o_buf[window]
    keep.wait()


def forward(backs, depth, where, sets, mix, ins, downs):
    rows, half = sets[0][0].shape[1:]
    width = ins[0].shape[1]
    total = 2 * rows * len(backs)
    flat = [piece for pieces in sets for piece in pieces]
    vmem = pl.BlockSpec(memory_space=pltpu.VMEM)
    hbm = pl.BlockSpec(memory_space=pl.ANY)
    return pl.pallas_call(
        functools.partial(forward_kernel, backs, depth, len(sets)),
        out_shape=tuple([jax.ShapeDtypeStruct((len(backs), rows, half), BF16)] * 4)
        + (
            jax.ShapeDtypeStruct((total, CORES * width), F32),
            jax.ShapeDtypeStruct((total, 2 * half), BF16),
        ),
        in_specs=[pl.BlockSpec(memory_space=pltpu.SMEM)] + [vmem] * (len(flat) + 5),
        out_specs=(vmem,) * 5 + (hbm,),
        scratch_shapes=[
            pltpu.VMEM((total, 2 * half), BF16),
            pltpu.VMEM((total, 2 * half), BF16),
            pltpu.SemaphoreType.DMA,
        ],
        compiler_params=pltpu.CompilerParams(vmem_limit_bytes=14 << 20),
        cost_estimate=pl.CostEstimate(
            flops=2 * total * half * width * 6, bytes_accessed=12 * total * half, transcendentals=total * width
        ),
    )(where, *flat, mix, *ins, *downs)


def backward_kernel(backs, depth, where_ref, *refs):
    count = len(backs)
    pairs, fars, refs = refs[:count], refs[count : 2 * count], refs[2 * count :]
    pre_ref, mix_ref, downs, refs = refs[0], refs[1], refs[2:4], refs[4:]
    cot_ref, hid_ref, both_ref, c_buf, h_buf, g_buf, sems = refs
    rows, half = pairs[0].shape[1:]
    for member in range(count):
        pieces = (pairs[member].at[0], pairs[member].at[1], fars[member].at[0], fars[member].at[1])
        for window, piece in zip(piece_windows(where_ref, member, rows, half), pieces):
            c_buf[window] = piece[...]
    copies = [pltpu.make_async_copy(c_buf, cot_ref, sems.at[CORES, 0])]
    copies[0].start()
    width = pre_ref.shape[1] // 2
    units = width // 2
    for slot in range(CORES):
        weights = row_weights(mix_ref, where_ref, backs, depth, slot)
        hidden_cot = weights * dot_columns(c_buf[...], downs[slot][...])
        gate = pre_ref[:, slot * width : slot * width + units]
        up = pre_ref[:, slot * width + units : (slot + 1) * width]
        sigma = jax.nn.sigmoid(gate)
        silu = gate * sigma
        h_buf[slot] = (weights * (silu * up)).astype(BF16)
        slope = sigma * (1.0 + gate * (1.0 - sigma))
        g_buf[slot, :, :units] = (hidden_cot * up * slope).astype(BF16)
        g_buf[slot, :, units:] = (hidden_cot * silu).astype(BF16)
        for number, (buf, to) in enumerate(((h_buf, hid_ref), (g_buf, both_ref))):
            copies.append(pltpu.make_async_copy(buf.at[slot], to.at[slot], sems.at[slot, number]))
            copies[-1].start()
    for copy in copies:
        copy.wait()


def backward(backs, depth, where, pairs, fars, pre, mix, downs):
    rows, half = pairs[0].shape[1:]
    width = pre.shape[1] // 2
    total = 2 * rows * len(backs)
    vmem = pl.BlockSpec(memory_space=pltpu.VMEM)
    hbm = pl.BlockSpec(memory_space=pl.ANY)
    return pl.pallas_call(
        functools.partial(backward_kernel, backs, depth),
        out_shape=(
            jax.ShapeDtypeStruct((total, 2 * half), BF16),
            jax.ShapeDtypeStruct((CORES, total, width // 2), BF16),
            jax.ShapeDtypeStruct((CORES, total, width), BF16),
        ),
        in_specs=[pl.BlockSpec(memory_space=pltpu.SMEM)] + [vmem] * (2 * len(backs) + 4),
        out_specs=(hbm,) * 3,
        scratch_shapes=[
            pltpu.VMEM((total, 2 * half), BF16),
            pltpu.VMEM((CORES, total, width // 2), BF16),
            pltpu.VMEM((CORES, total, width), BF16),
            pltpu.SemaphoreType.DMA((CORES + 1, 2)),
        ],
        compiler_params=pltpu.CompilerParams(vmem_limit_bytes=12 << 20),
        cost_estimate=pl.CostEstimate(
            flops=2 * total * half * width * 2, bytes_accessed=20 * total * half, transcendentals=total * width
        ),
    )(where, *pairs, *fars, pre, mix, *downs)


def grads_kernel(added, left_ref, right_ref, *refs):
    left = left_ref[...] if left_ref.ndim == 2 else left_ref[0]
    right = right_ref[...] if right_ref.ndim == 2 else right_ref[0]
    grads = dot_rows(left, right)
    for ref in refs[:added]:
        grads += ref[...].astype(F32)
    outs = refs[added:]
    columns = outs[0].shape[1]
    for number, ref in enumerate(outs):
        ref[...] = grads[:, number * columns : (number + 1) * columns].astype(ref.dtype)


def in_grads(slot, rows_ref, both, add, kinds):
    total, features = rows_ref.shape
    width = both.shape[2]
    tile = min(TILE, features)

    def tall(columns):
        return pl.BlockSpec((tile, columns), lambda i: (i, 0))

    columns = width // len(kinds)
    return pl.pallas_call(
        functools.partial(grads_kernel, len(add)),
        grid=(features // tile,),
        out_shape=tuple(jax.ShapeDtypeStruct((features, columns), kind) for kind in kinds),
        in_specs=[
            pl.BlockSpec((total, tile), lambda i: (0, i)),
            pl.BlockSpec((1, total, width), lambda i: (slot, 0, 0)),
        ]
        + [tall(width)] * len(add),
        out_specs=tuple(tall(columns) for _ in kinds),
        compiler_params=pltpu.CompilerParams(vmem_limit_bytes=20 << 20),
        cost_estimate=pl.CostEstimate(
            flops=2 * total * features * width, bytes_accessed=2 * features * (total + width), transcendentals=0
        ),
    )(rows_ref, both, *add)


def down_grads(slot, cot, hid, add, kind):
    total, features = cot.shape
    units = hid.shape[2]
    tile = min(TILE, features)
    flat = pl.BlockSpec((units, tile), lambda i: (0, i))
    return pl.pallas_call(
        functools.partial(grads_kernel, len(add)),
        grid=(features // tile,),
        out_shape=(jax.ShapeDtypeStruct((units, features), kind),),
        in_specs=[
            pl.BlockSpec((1, total, units), lambda i: (slot, 0, 0)),
            pl.BlockSpec((total, tile), lambda i: (0, i)),
        ]
        + [flat] * len(add),
        out_specs=(flat,),
        compiler_params=pltpu.CompilerParams(vmem_limit_bytes=16 << 20),
        cost_estimate=pl.CostEstimate(
            flops=2 * total * features * units, bytes_accessed=2 * features * (total + units), transcendentals=0
        ),
    )(hid, cot, *add)


def joint_grads_kernel(slots, added, splits, rows_ref, cot_ref, *refs):
    given = 2 + 2 * added
    outs = refs[given * slots :]
    for slot in range(slots):
        both_ref, hid_ref, *adds = refs[given * slot : given * (slot + 1)]
        results = outs[(splits + 1) * slot : (splits + 1) * (slot + 1)]
        grads = dot_rows(rows_ref[...], both_ref[0])
        for ref in adds[:added]:
            grads += ref[...].astype(F32)
        columns = results[0].shape[1]
        for number, ref in enumerate(results[:splits]):
            ref[...] = grads[:, number * columns : (number + 1) * columns].astype(ref.dtype)
        grads = dot_rows(hid_ref[0], cot_ref[...])
        for ref in adds[added:]:
            grads += ref[...].astype(F32)
        results[splits][...] = grads.astype(results[splits].dtype)


def joint_grads(slots, rows_ref, both, cot, hid, in_adds, down_adds, splits, kind):
    total, features = rows_ref.shape
    units, width = hid.shape[2], both.shape[2]
    tile = min(TILE // 2, features)
    added = len(in_adds[0])
    columns = width // splits

    def tall(columns):
        return pl.BlockSpec((tile, columns), lambda i: (i, 0))

    def whole(slot, columns):
        return pl.BlockSpec((1, total, columns), lambda i: (slot, 0, 0))

    flat = pl.BlockSpec((units, tile), lambda i: (0, i))
    some = pl.BlockSpec((total, tile), lambda i: (0, i))
    operands, in_specs, out_shape, out_specs = [rows_ref, cot], [some, some], [], []
    for number, slot in enumerate(slots):
        operands += [both, hid, *in_adds[number], *down_adds[number]]
        in_specs += [whole(slot, width), whole(slot, units)] + [tall(width)] * added + [flat] * added
        out_shape += [jax.ShapeDtypeStruct((features, columns), kind)] * splits
        out_shape += [jax.ShapeDtypeStruct((units, features), kind)]
        out_specs += [tall(columns)] * splits + [flat]
    return pl.pallas_call(
        functools.partial(joint_grads_kernel, len(slots), added, splits),
        grid=(features // tile,),
        out_shape=tuple(out_shape),
        in_specs=in_specs,
        out_specs=tuple(out_specs),
        compiler_params=pltpu.CompilerParams(vmem_limit_bytes=16 << 20),
        cost_estimate=pl.CostEstimate(
            flops=2 * total * features * (width + units) * len(slots),
            bytes_accessed=4 * features * (total + (width + units) * len(slots)),
            transcendentals=0,
        ),
    )(*operands)


def gather_plan(tokens, cotangent, routes, gate_probs, matching, gate_weight, up_weight, down_weight):
    expert_count = lax.axis_size("expert")
    depth, shift, swap, first, second = moves(expert_count)

    def send(value, pairs):
        return lax.ppermute(value, AXES, pairs)

    rows, _ = tokens.shape
    y, at = lax.axis_index("dp"), lax.axis_index("expert")
    where = jnp.stack([y, at // (SIDE * CORES), (at // CORES) % SIDE, at % CORES]).astype(jnp.int32)

    down = down_weight[0]
    downs = (down, send(down, swap))
    in_weight = jnp.concatenate([gate_weight[0], up_weight[0]], axis=1)
    ins = (in_weight, send(in_weight, swap))

    groups = [tuple(range(at, min(at + GROUP, depth))) for at in range(0, depth, GROUP)]

    along = [tokens]
    for _ in range(1, depth):
        along.append(send(along[-1], shift[1]))
    around = []
    for piece in along:
        piece = piece[None]
        a = send(piece, first)
        b = send(piece, second)
        d = send(a, second)
        around.append((piece, a, b, d))
    sets = [[around[back] for back in backs] for backs in groups]

    pairs = [jnp.stack([cotangent, send(cotangent, first)])]
    late = depth // 2
    for back in range(1, depth):
        if back > late:
            pairs.append(send(pairs[0], shift[back - depth]))
        else:
            pairs.append(send(pairs[-1], shift[1]))
    fars = []
    for back, pair in enumerate(pairs):
        if back in ALONG:
            source, by = ALONG[back]
            fars.append(send(fars[source], shift[by]))
        else:
            fars.append(send(pair, second))

    mix = gate_probs / jnp.sum(gate_probs, axis=1, keepdims=True)
    hit = routes[:, :, None] == jnp.arange(matching.shape[0], dtype=jnp.int32)
    host = jnp.sum(jnp.where(hit, matching, 0), axis=2)
    slots = jnp.arange(expert_count, dtype=jnp.int32)
    slots = (slots[:, None] // CORES * CORES + jnp.arange(CORES, dtype=jnp.int32)).reshape(-1)
    per_slot = jnp.sum(jnp.where(host[None] == slots[:, None, None], mix[None], 0.0), axis=2)
    mix = lax.all_to_all(per_slot, "expert", split_axis=0, concat_axis=0, tiled=True)
    mix = mix.reshape(CORES * expert_count, rows)

    kept_rows, pres, out = [], [], None
    for number, backs in enumerate(groups):
        *got, pre, kept = forward(backs, depth, where, sets[number], mix, ins, downs)
        pres.append(pre)
        kept_rows.append(kept)
        own, a, b, d = got
        d = send(d, second)
        b = send(b, second)
        a = (a.astype(F32) + d).astype(BF16)
        a = send(a, first)
        own = own.astype(F32) + a + b
        for member, back in enumerate(backs):
            part = own[member]
            if back:
                part = send(part.astype(BF16), shift[-back]).astype(F32)
            out = part if out is None else out + part

    in_sums, down_sums = [[], []], [[], []]
    for number, backs in enumerate(groups):
        some = slice(backs[0], backs[-1] + 1)
        cot, hid, both = backward(
            backs, depth, where, pairs[some], fars[some], pres[number], mix, downs
        )
        if number == len(groups) - 1:
            break
        sums = joint_grads((0, 1), kept_rows[number], both, cot, hid, in_sums, down_sums, 1, F32)
        in_sums, down_sums = [[sums[0]], [sums[2]]], [[sums[1]], [sums[3]]]
    (in_got,) = in_grads(1, kept_rows[-1], both, in_sums[1], (BF16,))
    in_got = send(in_got, swap)
    (down_got,) = down_grads(1, cot, hid, down_sums[1], BF16)
    down_got = send(down_got, swap)
    gate_grad, up_grad = in_grads(0, kept_rows[-1], both, [*in_sums[0], in_got], (BF16, BF16))
    (down_grad,) = down_grads(0, cot, hid, [*down_sums[0], down_got], BF16)
    out = out.astype(BF16)
    return out, gate_grad[None], up_grad[None], down_grad[None]


def solution(mesh):
    experts = mesh.shape["expert"]
    square = mesh.shape["dp"] == 2 and experts % (SIDE * CORES) == 0

    def on_device(*args):
        dense = 2 * args[2].shape[1] >= experts
        if not (square and dense):
            return exchange_plan(*args)
        return gather_plan(*args)

    placed = (
        P("expert", "dp"),
        P("expert", "dp"),
        P("expert", None),
        P("expert", None),
        P(),
        P("expert", None, "dp"),
        P("expert", None, "dp"),
        P("expert", "dp", None),
    )
    return jax.shard_map(
        on_device,
        mesh=mesh,
        in_specs=placed,
        out_specs=(
            P("expert", "dp"),
            P("expert", None, "dp"),
            P("expert", None, "dp"),
            P("expert", "dp", None),
        ),
        check_vma=False,
    )
```

```python
import functools

import jax
import jax.numpy as jnp
from jax import lax
from jax.experimental import pallas as pl
from jax.experimental.pallas import tpu as pltpu
from jax.sharding import PartitionSpec as P


AXES = ("dp", "expert")
CORES = 2
SIDE = 2
GROUP = 2
ALONG = {3: (0, -1), 2: (1, 1)}
TILE = 512
F32 = jnp.float32
BF16 = jnp.bfloat16


def exchange_plan(tokens, cotangent, routes, gate_probs, matching, gate_weight, up_weight, down_weight):
    expert_count = lax.axis_size("expert")
    token_count, fan_out = routes.shape
    capacity = max(2, token_count * fan_out * 9 // (8 * expert_count))
    route_count = token_count * fan_out
    mix_weights = gate_probs / jnp.sum(gate_probs, axis=1, keepdims=True)
    flat_routes = routes.reshape(-1)
    expert_hit = flat_routes[:, None] == jnp.arange(matching.shape[0], dtype=jnp.int32)[None, :]
    host_of = jnp.sum(jnp.where(expert_hit, matching[None, :], 0), axis=1)
    host_hit = (host_of[:, None] == jnp.arange(expert_count, dtype=jnp.int32)[None, :]).astype(
        jnp.int32
    )
    running = jnp.cumsum(host_hit, axis=0)
    slot_rank = jnp.sum((running - 1) * host_hit, axis=1)
    position = host_of * capacity + slot_rank
    slot_table = (
        jnp.full((expert_count * capacity,), route_count, jnp.int32)
        .at[position]
        .set(jnp.arange(route_count, dtype=jnp.int32))
    )
    filled = slot_table < route_count
    route_ids = jnp.minimum(slot_table, route_count - 1)
    token_ids = jnp.where(filled, route_ids // fan_out, token_count)
    clamped_ids = route_ids // fan_out
    slot_mix = jnp.where(filled, jnp.take(mix_weights.reshape(-1), route_ids), 0.0)
    recv_rows = lax.all_to_all(
        jnp.take(tokens, token_ids, axis=0, mode="fill", fill_value=0),
        "expert",
        split_axis=0,
        concat_axis=0,
        tiled=True,
    )
    gathered = jnp.take(cotangent, clamped_ids, axis=0)
    recv_cot = lax.all_to_all(
        (slot_mix[:, None] * gathered.astype(jnp.float32)).astype(jnp.bfloat16),
        "expert",
        split_axis=0,
        concat_axis=0,
        tiled=True,
    )
    inputs, out_cot = (
        lax.all_gather(recv_rows, "dp", axis=1, tiled=True),
        lax.all_gather(recv_cot, "dp", axis=1, tiled=True),
    )
    gate_pre = jnp.dot(inputs, gate_weight[0], preferred_element_type=jnp.float32)
    up_pre = jnp.dot(inputs, up_weight[0], preferred_element_type=jnp.float32)
    sigma_gate = jax.nn.sigmoid(gate_pre)
    silu_gate = gate_pre * sigma_gate
    hidden = (silu_gate * up_pre).astype(jnp.bfloat16)
    partial_out = jnp.dot(hidden, down_weight[0], preferred_element_type=jnp.float32)
    contract_rows = (((0,), (0,)), ((), ()))
    down_grad = lax.dot_general(
        hidden, out_cot, contract_rows, preferred_element_type=jnp.float32
    ).astype(jnp.bfloat16)
    hidden_cot = lax.dot_general(
        out_cot, down_weight[0], (((1,), (1,)), ((), ())), preferred_element_type=jnp.float32
    )
    slope = sigma_gate * (1.0 + gate_pre * (1.0 - sigma_gate))
    gate_cot = (hidden_cot * up_pre * slope).astype(jnp.bfloat16)
    up_cot = (hidden_cot * silu_gate).astype(jnp.bfloat16)
    gate_grad = lax.dot_general(
        inputs, gate_cot, contract_rows, preferred_element_type=jnp.float32
    ).astype(jnp.bfloat16)
    up_grad = lax.dot_general(
        inputs, up_cot, contract_rows, preferred_element_type=jnp.float32
    ).astype(jnp.bfloat16)
    summed = lax.psum_scatter(
        partial_out.astype(jnp.bfloat16), "dp", scatter_dimension=1, tiled=True
    )
    merged = lax.all_to_all(summed, "expert", split_axis=0, concat_axis=0, tiled=True)
    half_width = merged.shape[1]
    expert_out = jnp.take(merged, position, axis=0).reshape(token_count, fan_out, half_width)
    layer_out = jnp.sum(mix_weights[:, :, None] * expert_out.astype(jnp.float32), axis=1).astype(
        jnp.bfloat16
    )
    return (layer_out, gate_grad[None], up_grad[None], down_grad[None])


def moves(expert_count):
    depth = expert_count // (SIDE * CORES)

    def table(step):
        pairs = []
        for y in range(2):
            for z in range(depth):
                for x in range(SIDE):
                    for core in range(CORES):
                        ty, tz, tx, tcore = step(y, z, x, core)
                        pairs.append(
                            (
                                y * expert_count + (z * SIDE + x) * CORES + core,
                                ty * expert_count + (tz * SIDE + tx) * CORES + tcore,
                            )
                        )
        return pairs

    shift = {
        by: table(lambda y, z, x, core, by=by: (y, (z + by) % depth, x, core))
        for by in range(1 - depth, depth)
        if by
    }
    swap = table(lambda y, z, x, core: (y, z, x, 1 - core))
    first = table(lambda y, z, x, core: (y, z, 1 - x, core) if core == 0 else (1 - y, z, x, core))
    second = table(lambda y, z, x, core: (1 - y, z, x, core) if core == 0 else (y, z, 1 - x, core))
    return depth, shift, swap, first, second


def dot(a, b):
    return jnp.dot(a, b, preferred_element_type=F32)


def dot_rows(a, b):
    return lax.dot_general(a, b, (((0,), (0,)), ((), ())), preferred_element_type=F32)


def dot_columns(a, b):
    return lax.dot_general(a, b, (((1,), (1,)), ((), ())), preferred_element_type=F32)


def piece_windows(where_ref, member, rows, half):
    y, core = where_ref[0], where_ref[3]

    def window(lower, other):
        side = jnp.where(other == 1, 1 - y, y)
        return (
            pl.ds(pl.multiple_of((2 * member + lower) * rows, rows), rows),
            pl.ds(pl.multiple_of(side * half, half), half),
        )

    return window(0, 0), window(1 - core, core), window(core, 1 - core), window(1, 1)


def row_weights(mix_ref, where_ref, backs, depth, slot):
    core, x = where_ref[3], where_ref[2]
    parity = core if slot == 0 else 1 - core
    rows = mix_ref.shape[1]
    down = lax.broadcasted_iota(jnp.int32, (rows, rows), 0)
    along = lax.broadcasted_iota(jnp.int32, (rows, rows), 1)
    columns = []
    for back in backs:
        z = lax.rem(where_ref[1] + depth - back, depth)
        for across in (x, 1 - x):
            block = (z * SIDE + across) * CORES + core
            row = mix_ref[pl.ds(block * CORES + parity, 1), :]
            columns.append(jnp.sum(jnp.where(down == along, row, 0.0), axis=1, keepdims=True))
    return jnp.concatenate(columns, axis=0)


def forward_kernel(backs, depth, sets, where_ref, *refs):
    pieces, refs = refs[: 4 * sets], refs[4 * sets :]
    mix_ref, ins, downs, refs = refs[0], refs[1:3], refs[3:5], refs[5:]
    outs, pre_ref, rows_ref, x_buf, o_buf, sem = refs[:4], refs[4], refs[5], refs[6], refs[7], refs[8]
    rows, half = pieces[0].shape[1:]
    member = 0
    for number in range(sets):
        group = pieces[4 * number : 4 * number + 4]
        for inner in range(group[0].shape[0]):
            for window, piece in zip(piece_windows(where_ref, member, rows, half), group):
                x_buf[window] = piece[inner]
            member += 1
    keep = pltpu.make_async_copy(x_buf, rows_ref, sem)
    keep.start()
    width = ins[0].shape[1]
    units = width // 2
    cut = width * 2 // 3
    for slot in range(CORES):
        pre_ref[:, slot * width : slot * width + cut] = dot(x_buf[...], ins[slot][:, :cut])
    last = dot(x_buf[...], jnp.concatenate([ins[0][:, cut:], ins[1][:, cut:]], axis=1))
    pre_ref[:, cut:width] = last[:, : width - cut]
    pre_ref[:, width + cut :] = last[:, width - cut :]
    hiddens = []
    for slot in range(CORES):
        gate = pre_ref[:, slot * width : slot * width + units]
        up = pre_ref[:, slot * width + units : (slot + 1) * width]
        weights = row_weights(mix_ref, where_ref, backs, depth, slot)
        hiddens.append((weights * (gate * jax.nn.sigmoid(gate) * up)).astype(BF16))
    o_buf[...] = dot(
        jnp.concatenate(hiddens, axis=1), jnp.concatenate([downs[0][...], downs[1][...]], axis=0)
    ).astype(BF16)
    for member in range(len(backs)):
        for window, ref in zip(piece_windows(where_ref, member, rows, half), outs):
            ref[member] = o_buf[window]
    keep.wait()


def forward(backs, depth, where, sets, mix, ins, downs):
    rows, half = sets[0][0].shape[1:]
    width = ins[0].shape[1]
    total = 2 * rows * len(backs)
    flat = [piece for pieces in sets for piece in pieces]
    vmem = pl.BlockSpec(memory_space=pltpu.VMEM)
    hbm = pl.BlockSpec(memory_space=pl.ANY)
    return pl.pallas_call(
        functools.partial(forward_kernel, backs, depth, len(sets)),
        out_shape=tuple([jax.ShapeDtypeStruct((len(backs), rows, half), BF16)] * 4)
        + (
            jax.ShapeDtypeStruct((total, CORES * width), F32),
            jax.ShapeDtypeStruct((total, 2 * half), BF16),
        ),
        in_specs=[pl.BlockSpec(memory_space=pltpu.SMEM)] + [vmem] * (len(flat) + 5),
        out_specs=(vmem,) * 5 + (hbm,),
        scratch_shapes=[
            pltpu.VMEM((total, 2 * half), BF16),
            pltpu.VMEM((total, 2 * half), BF16),
            pltpu.SemaphoreType.DMA,
        ],
        compiler_params=pltpu.CompilerParams(vmem_limit_bytes=14 << 20),
        cost_estimate=pl.CostEstimate(
            flops=2 * total * half * width * 6, bytes_accessed=12 * total * half, transcendentals=total * width
        ),
    )(where, *flat, mix, *ins, *downs)


def backward_kernel(backs, depth, where_ref, *refs):
    count = len(backs)
    pairs, fars, refs = refs[:count], refs[count : 2 * count], refs[2 * count :]
    pre_ref, mix_ref, downs, refs = refs[0], refs[1], refs[2:4], refs[4:]
    cot_ref, hid_ref, both_ref, c_buf, h_buf, g_buf, sems = refs
    rows, half = pairs[0].shape[1:]
    for member in range(count):
        pieces = (pairs[member].at[0], pairs[member].at[1], fars[member].at[0], fars[member].at[1])
        for window, piece in zip(piece_windows(where_ref, member, rows, half), pieces):
            c_buf[window] = piece[...]
    copies = [pltpu.make_async_copy(c_buf, cot_ref, sems.at[CORES, 0])]
    copies[0].start()
    width = pre_ref.shape[1] // 2
    units = width // 2
    products = dot_columns(c_buf[...], jnp.concatenate([downs[0][...], downs[1][...]], axis=0))
    for slot in range(CORES):
        weights = row_weights(mix_ref, where_ref, backs, depth, slot)
        hidden_cot = weights * products[:, slot * units : (slot + 1) * units]
        gate = pre_ref[:, slot * width : slot * width + units]
        up = pre_ref[:, slot * width + units : (slot + 1) * width]
        sigma = jax.nn.sigmoid(gate)
        silu = gate * sigma
        h_buf[slot] = (weights * (silu * up)).astype(BF16)
        slope = sigma * (1.0 + gate * (1.0 - sigma))
        g_buf[slot, :, :units] = (hidden_cot * up * slope).astype(BF16)
        g_buf[slot, :, units:] = (hidden_cot * silu).astype(BF16)
        for number, (buf, to) in enumerate(((h_buf, hid_ref), (g_buf, both_ref))):
            copies.append(pltpu.make_async_copy(buf.at[slot], to.at[slot], sems.at[slot, number]))
            copies[-1].start()
    for copy in copies:
        copy.wait()


def backward(backs, depth, where, pairs, fars, pre, mix, downs):
    rows, half = pairs[0].shape[1:]
    width = pre.shape[1] // 2
    total = 2 * rows * len(backs)
    vmem = pl.BlockSpec(memory_space=pltpu.VMEM)
    hbm = pl.BlockSpec(memory_space=pl.ANY)
    return pl.pallas_call(
        functools.partial(backward_kernel, backs, depth),
        out_shape=(
            jax.ShapeDtypeStruct((total, 2 * half), BF16),
            jax.ShapeDtypeStruct((CORES, total, width // 2), BF16),
            jax.ShapeDtypeStruct((CORES, total, width), BF16),
        ),
        in_specs=[pl.BlockSpec(memory_space=pltpu.SMEM)] + [vmem] * (2 * len(backs) + 4),
        out_specs=(hbm,) * 3,
        scratch_shapes=[
            pltpu.VMEM((total, 2 * half), BF16),
            pltpu.VMEM((CORES, total, width // 2), BF16),
            pltpu.VMEM((CORES, total, width), BF16),
            pltpu.SemaphoreType.DMA((CORES + 1, 2)),
        ],
        compiler_params=pltpu.CompilerParams(vmem_limit_bytes=12 << 20),
        cost_estimate=pl.CostEstimate(
            flops=2 * total * half * width * 2, bytes_accessed=20 * total * half, transcendentals=total * width
        ),
    )(where, *pairs, *fars, pre, mix, *downs)


def grads_kernel(added, left_ref, right_ref, *refs):
    left = left_ref[...] if left_ref.ndim == 2 else left_ref[0]
    right = right_ref[...] if right_ref.ndim == 2 else right_ref[0]
    grads = dot_rows(left, right)
    for ref in refs[:added]:
        grads += ref[...].astype(F32)
    outs = refs[added:]
    columns = outs[0].shape[1]
    for number, ref in enumerate(outs):
        ref[...] = grads[:, number * columns : (number + 1) * columns].astype(ref.dtype)


def in_grads(slot, rows_ref, both, add, kinds):
    total, features = rows_ref.shape
    width = both.shape[2]
    tile = min(TILE, features)

    def tall(columns):
        return pl.BlockSpec((tile, columns), lambda i: (i, 0))

    columns = width // len(kinds)
    return pl.pallas_call(
        functools.partial(grads_kernel, len(add)),
        grid=(features // tile,),
        out_shape=tuple(jax.ShapeDtypeStruct((features, columns), kind) for kind in kinds),
        in_specs=[
            pl.BlockSpec((total, tile), lambda i: (0, i)),
            pl.BlockSpec((1, total, width), lambda i: (slot, 0, 0)),
        ]
        + [tall(width)] * len(add),
        out_specs=tuple(tall(columns) for _ in kinds),
        compiler_params=pltpu.CompilerParams(vmem_limit_bytes=20 << 20),
        cost_estimate=pl.CostEstimate(
            flops=2 * total * features * width, bytes_accessed=2 * features * (total + width), transcendentals=0
        ),
    )(rows_ref, both, *add)


def down_grads(slot, cot, hid, add, kind):
    total, features = cot.shape
    units = hid.shape[2]
    tile = min(2 * TILE, features)
    flat = pl.BlockSpec((units, tile), lambda i: (0, i))
    return pl.pallas_call(
        functools.partial(grads_kernel, len(add)),
        grid=(features // tile,),
        out_shape=(jax.ShapeDtypeStruct((units, features), kind),),
        in_specs=[
            pl.BlockSpec((1, total, units), lambda i: (slot, 0, 0)),
            pl.BlockSpec((total, tile), lambda i: (0, i)),
        ]
        + [flat] * len(add),
        out_specs=(flat,),
        compiler_params=pltpu.CompilerParams(vmem_limit_bytes=16 << 20),
        cost_estimate=pl.CostEstimate(
            flops=2 * total * features * units, bytes_accessed=2 * features * (total + units), transcendentals=0
        ),
    )(hid, cot, *add)


def joint_grads_kernel(slots, added, splits, rows_ref, cot_ref, *refs):
    given = 2 + 2 * added
    outs = refs[given * slots :]
    for slot in range(slots):
        both_ref, hid_ref, *adds = refs[given * slot : given * (slot + 1)]
        results = outs[(splits + 1) * slot : (splits + 1) * (slot + 1)]
        grads = dot_rows(rows_ref[...], both_ref[0])
        for ref in adds[:added]:
            grads += ref[...].astype(F32)
        columns = results[0].shape[1]
        for number, ref in enumerate(results[:splits]):
            ref[...] = grads[:, number * columns : (number + 1) * columns].astype(ref.dtype)
        grads = dot_rows(hid_ref[0], cot_ref[...])
        for ref in adds[added:]:
            grads += ref[...].astype(F32)
        results[splits][...] = grads.astype(results[splits].dtype)


def joint_grads(slots, rows_ref, both, cot, hid, in_adds, down_adds, splits, kind):
    total, features = rows_ref.shape
    units, width = hid.shape[2], both.shape[2]
    tile = min(TILE // 2, features)
    added = len(in_adds[0])
    columns = width // splits

    def tall(columns):
        return pl.BlockSpec((tile, columns), lambda i: (i, 0))

    def whole(slot, columns):
        return pl.BlockSpec((1, total, columns), lambda i: (slot, 0, 0))

    flat = pl.BlockSpec((units, tile), lambda i: (0, i))
    some = pl.BlockSpec((total, tile), lambda i: (0, i))
    operands, in_specs, out_shape, out_specs = [rows_ref, cot], [some, some], [], []
    for number, slot in enumerate(slots):
        operands += [both, hid, *in_adds[number], *down_adds[number]]
        in_specs += [whole(slot, width), whole(slot, units)] + [tall(width)] * added + [flat] * added
        out_shape += [jax.ShapeDtypeStruct((features, columns), kind)] * splits
        out_shape += [jax.ShapeDtypeStruct((units, features), kind)]
        out_specs += [tall(columns)] * splits + [flat]
    return pl.pallas_call(
        functools.partial(joint_grads_kernel, len(slots), added, splits),
        grid=(features // tile,),
        out_shape=tuple(out_shape),
        in_specs=in_specs,
        out_specs=tuple(out_specs),
        compiler_params=pltpu.CompilerParams(vmem_limit_bytes=16 << 20),
        cost_estimate=pl.CostEstimate(
            flops=2 * total * features * (width + units) * len(slots),
            bytes_accessed=4 * features * (total + (width + units) * len(slots)),
            transcendentals=0,
        ),
    )(*operands)


def gather_plan(tokens, cotangent, routes, gate_probs, matching, gate_weight, up_weight, down_weight):
    expert_count = lax.axis_size("expert")
    depth, shift, swap, first, second = moves(expert_count)

    def send(value, pairs):
        return lax.ppermute(value, AXES, pairs)

    rows, _ = tokens.shape
    y, at = lax.axis_index("dp"), lax.axis_index("expert")
    where = jnp.stack([y, at // (SIDE * CORES), (at // CORES) % SIDE, at % CORES]).astype(jnp.int32)

    down = down_weight[0]
    downs = (down, send(down, swap))
    in_weight = jnp.concatenate([gate_weight[0], up_weight[0]], axis=1)
    ins = (in_weight, send(in_weight, swap))

    groups = [tuple(range(at, min(at + GROUP, depth))) for at in range(0, depth, GROUP)]

    along = [tokens]
    for _ in range(1, depth):
        along.append(send(along[-1], shift[1]))
    around = []
    for piece in along:
        piece = piece[None]
        a = send(piece, first)
        b = send(piece, second)
        d = send(a, second)
        around.append((piece, a, b, d))
    sets = [[around[back] for back in backs] for backs in groups]

    pairs = [jnp.stack([cotangent, send(cotangent, first)])]
    late = depth // 2
    for back in range(1, depth):
        if back > late:
            pairs.append(send(pairs[0], shift[back - depth]))
        else:
            pairs.append(send(pairs[-1], shift[1]))
    fars = []
    for back, pair in enumerate(pairs):
        if back in ALONG:
            source, by = ALONG[back]
            fars.append(send(fars[source], shift[by]))
        else:
            fars.append(send(pair, second))

    mix = gate_probs / jnp.sum(gate_probs, axis=1, keepdims=True)
    hit = routes[:, :, None] == jnp.arange(matching.shape[0], dtype=jnp.int32)
    host = jnp.sum(jnp.where(hit, matching, 0), axis=2)
    slots = jnp.arange(expert_count, dtype=jnp.int32)
    slots = (slots[:, None] // CORES * CORES + jnp.arange(CORES, dtype=jnp.int32)).reshape(-1)
    per_slot = jnp.sum(jnp.where(host[None] == slots[:, None, None], mix[None], 0.0), axis=2)
    mix = lax.all_to_all(per_slot, "expert", split_axis=0, concat_axis=0, tiled=True)
    mix = mix.reshape(CORES * expert_count, rows)

    kept_rows, pres, out = [], [], None
    for number, backs in enumerate(groups):
        *got, pre, kept = forward(backs, depth, where, sets[number], mix, ins, downs)
        pres.append(pre)
        kept_rows.append(kept)
        own, a, b, d = got
        d = send(d, second)
        b = send(b, second)
        a = (a.astype(F32) + d).astype(BF16)
        a = send(a, first)
        own = own.astype(F32) + a + b
        for member, back in enumerate(backs):
            part = own[member]
            if back:
                part = send(part.astype(BF16), shift[-back]).astype(F32)
            out = part if out is None else out + part

    in_sums, down_sums = [[], []], [[], []]
    for number, backs in enumerate(groups):
        some = slice(backs[0], backs[-1] + 1)
        cot, hid, both = backward(
            backs, depth, where, pairs[some], fars[some], pres[number], mix, downs
        )
        if number == len(groups) - 1:
            break
        sums = joint_grads((0, 1), kept_rows[number], both, cot, hid, in_sums, down_sums, 1, F32)
        in_sums, down_sums = [[sums[0]], [sums[2]]], [[sums[1]], [sums[3]]]
    (in_got,) = in_grads(1, kept_rows[-1], both, in_sums[1], (BF16,))
    in_got = send(in_got, swap)
    (down_got,) = down_grads(1, cot, hid, down_sums[1], BF16)
    down_got = send(down_got, swap)
    gate_grad, up_grad = in_grads(0, kept_rows[-1], both, [*in_sums[0], in_got], (BF16, BF16))
    (down_grad,) = down_grads(0, cot, hid, [*down_sums[0], down_got], BF16)
    out = out.astype(BF16)
    return out, gate_grad[None], up_grad[None], down_grad[None]


def solution(mesh):
    experts = mesh.shape["expert"]
    square = mesh.shape["dp"] == 2 and experts % (SIDE * CORES) == 0

    def on_device(*args):
        dense = 2 * args[2].shape[1] >= experts
        if not (square and dense):
            return exchange_plan(*args)
        return gather_plan(*args)

    placed = (
        P("expert", "dp"),
        P("expert", "dp"),
        P("expert", None),
        P("expert", None),
        P(),
        P("expert", None, "dp"),
        P("expert", None, "dp"),
        P("expert", "dp", None),
    )
    return jax.shard_map(
        on_device,
        mesh=mesh,
        in_specs=placed,
        out_specs=(
            P("expert", "dp"),
            P("expert", None, "dp"),
            P("expert", None, "dp"),
            P("expert", "dp", None),
        ),
        check_vma=False,
    )
```
